32 devices in a mesh: row: 4 (over y, core), col: 8 (over z, x).
Axes of the slice: x: 2, y: 2, z: 4, core: 2. Of those that a mesh axis runs over, the one named last changes fastest.
Arguments:
- user_factors: float32 [8192, 128], P('row'), may hold values from -6 to 6
- item_factors: float32 [32768, 128], P(('row', 'col')), may hold values from -0.03125 to 0.03125
- fetch_list: int32 [4, 8, 32, 1], P('row', 'col'), may hold values from 0 to 7
- tile_user: int32 [4, 8, 32], P('row', 'col'), may hold values from 0 to 15
- tile_slot: int32 [4, 8, 32], P('row', 'col'), may hold values from 0 to 31
- entry_row: int32 [4, 8, 32, 512], P('row', 'col'), may hold values from 0 to 127
- entry_col: int32 [4, 8, 32, 512], P('row', 'col'), may hold values from 0 to 127
- entry_count: int32 [4, 8, 32, 512], P('row', 'col'), may hold values from 1 to 8
- tile_count: int32 [4, 8], P('row', 'col'), may hold values from 4 to 32, as said below
Outputs:
- solved: float32 [8192, 128], P('row')
The draws below stay inside these ranges and needn't reach their ends.
Inputs may be any that keep to these rules, and one draw needn't show every extreme that they name: `tile_count`: at least 4 tiles live on every device; some device has all 32 live in every draw.
All inputs are finite; a program needn't handle non-finite values.
Results may differ from the reference program's by a relative error of at most 0.0003.
Values sent between devices are 32-bit elements; how exact they have to be, the bound alone decides.
No kernel may reach another device: no remote copies, remote signals or barrier semaphores. Data moves between devices by JAX's collectives and lax.ppermute only.
A program may use at most 128 MiB of HBM per device.

```python
import jax
import jax.numpy as jnp
from jax import lax

K = 128
BLOCK = 128
UB_DEV = 16
IB_DEV = 8
TILES_DEV = 32
NNZ = 512
CAP = 1
ITERS = 3
USERS = 8192
ITEMS = 32768
SLOTS = 32
N_ROW = 4
N_COL = 8
DEVICES = 32


def draw_tile_count(key, part):
    first, second, third = jax.random.split(key, 3)
    power = jax.random.randint(first, (N_ROW, N_COL), 0, 4)
    divisor = jnp.array([1, 2, 4, 8], jnp.int32)[power]
    counts = TILES_DEV // divisor
    row_pick = jax.random.randint(second, (), 0, N_ROW)
    col_pick = jax.random.randint(third, (), 0, N_COL)
    return counts.at[row_pick, col_pick].set(TILES_DEV).astype(jnp.int32)


def set_ends(result, key, low, top_value):
    longest = result.shape.index(max(result.shape))
    spots = []
    for shift in (0, 1):
        where = [jax.random.randint(jax.random.fold_in(key, axis), (), 0, length) for axis, length in enumerate(result.shape)]
        where[longest] = (where[longest] + shift) % result.shape[longest]
        spots.append(tuple(where))
    return result.at[spots[0]].set(low).at[spots[1]].set(top_value)


def block_levels(key, dims, shards, least, top_value):
    gain = 1.0
    for position, shards_of in shards:
        heights = jax.random.uniform(jax.random.fold_in(jax.random.fold_in(key, 6), position), (shards_of,), jnp.float32, least / len(shards), top_value / len(shards))
        gain = gain * jnp.repeat(jnp.exp(heights), dims[position] // shards_of).reshape((-1,) + (1,) * (len(dims) - 1 - position))
    return gain


def bell_draw(stream_key, dims, width, most, pieces=(), kind=jnp.bfloat16):
    result = width * jax.random.normal(stream_key, dims, jnp.float32)
    if pieces:
        result = result * block_levels(stream_key, dims, pieces, -0.22, 0.18)
    return jnp.clip(result, -most, most).astype(kind)


def setup_inputs(seed: int = 0) -> dict:
    keys = jax.random.split(jax.random.key(seed), 10)
    user_factors = bell_draw(keys[0], (USERS, K), 1.0, 6.0, ((0, 4),), jnp.float32)
    item_factors = bell_draw(keys[1], (ITEMS, K), ITEMS ** -0.5, 0.03125, ((0, 32),), jnp.float32)
    fetch_list = set_ends(jax.random.randint(keys[2], (N_ROW, N_COL, DEVICES, CAP), 0, IB_DEV), jax.random.fold_in(keys[2], 1), 0, IB_DEV - 1).astype(jnp.int32)
    tile_user = set_ends(jax.random.randint(keys[3], (N_ROW, N_COL, TILES_DEV), 0, UB_DEV), jax.random.fold_in(keys[3], 1), 0, UB_DEV - 1).astype(jnp.int32)
    tile_slot = set_ends(jax.random.randint(keys[4], (N_ROW, N_COL, TILES_DEV), 0, SLOTS), jax.random.fold_in(keys[4], 1), 0, SLOTS - 1).astype(jnp.int32)
    entry_row = set_ends(jax.random.randint(keys[5], (N_ROW, N_COL, TILES_DEV, NNZ), 0, BLOCK), jax.random.fold_in(keys[5], 1), 0, BLOCK - 1).astype(jnp.int32)
    entry_col = set_ends(jax.random.randint(keys[6], (N_ROW, N_COL, TILES_DEV, NNZ), 0, BLOCK), jax.random.fold_in(keys[6], 1), 0, BLOCK - 1).astype(jnp.int32)
    entry_count = set_ends(jax.random.randint(keys[7], (N_ROW, N_COL, TILES_DEV, NNZ), 1, 9), jax.random.fold_in(keys[7], 1), 1, 8).astype(jnp.int32)
    tile_count = draw_tile_count(jax.random.fold_in(keys[9], 71), 0)
    return {"user_factors": user_factors, "item_factors": item_factors, "fetch_list": fetch_list, "tile_user": tile_user, "tile_slot": tile_slot, "entry_row": entry_row, "entry_col": entry_col, "entry_count": entry_count, "tile_count": tile_count}


HIGHEST = lax.Precision.HIGHEST
CONFIDENCE_SCALE = 40.0
RIDGE = 0.5
EPSILON = 1e-6


def reference(user_factors, item_factors, fetch_list, tile_user, tile_slot, entry_row, entry_col, entry_count, tile_count):
    gram = jnp.dot(item_factors.T, item_factors, precision=HIGHEST, preferred_element_type=jnp.float32)
    user_rows = UB_DEV * BLOCK
    starting = user_factors.reshape(N_ROW, user_rows, K)

    def one_shard(packed):
        start_point, fetched, users, slot_ids, rows_in, cols_in, counts, live = packed
        alive = (jnp.arange(TILES_DEV, dtype=jnp.int32)[None, :] < live[:, None]).astype(jnp.float32)
        owner = slot_ids // CAP
        member = slot_ids % CAP
        col_index = jnp.broadcast_to(jnp.arange(N_COL, dtype=jnp.int32)[:, None], owner.shape)
        local_id = fetched[col_index, owner, member]
        global_block = owner * IB_DEV + local_id
        item_index = (global_block[..., None] * BLOCK + cols_in).reshape(-1).astype(jnp.int32)
        user_index = (users[..., None] * BLOCK + rows_in).reshape(-1).astype(jnp.int32)
        excess = CONFIDENCE_SCALE * counts.astype(jnp.float32)
        weight_fit = (excess * alive[..., None]).reshape(-1)
        weight_rhs = ((1.0 + excess) * alive[..., None]).reshape(-1)
        picked = jnp.take(item_factors, item_index, axis=0)

        def apply_operator(vector):
            inner = jnp.sum(picked * jnp.take(vector, user_index, axis=0), axis=1)
            data = jax.ops.segment_sum((weight_fit * inner)[:, None] * picked, user_index, num_segments=user_rows)
            return data + jnp.dot(vector, gram, precision=HIGHEST, preferred_element_type=jnp.float32) + RIDGE * vector

        rhs = jax.ops.segment_sum(weight_rhs[:, None] * picked, user_index, num_segments=user_rows)
        iterate = start_point
        residual = rhs - apply_operator(iterate)
        direction = residual
        norm_now = jnp.sum(residual * residual, axis=1, keepdims=True)
        for iteration in range(ITERS):
            image = apply_operator(direction)
            alpha = norm_now / (jnp.sum(direction * image, axis=1, keepdims=True) + EPSILON)
            iterate = iterate + alpha * direction
            residual = residual - alpha * image
            norm_next = jnp.sum(residual * residual, axis=1, keepdims=True)
            direction = residual + (norm_next / (norm_now + EPSILON)) * direction
            norm_now = norm_next
        return iterate

    solved = lax.map(one_shard, (starting, fetch_list, tile_user, tile_slot, entry_row, entry_col, entry_count, tile_count))
    return solved.reshape(USERS, K)
```

```python
import jax
import jax.numpy as jnp
from jax import lax
from jax.experimental import pallas as pl
from jax.experimental.pallas import tpu as pltpu
from jax.sharding import PartitionSpec as P

K = 128
BLOCK = 128
CONFIDENCE_SCALE = 40.0
RIDGE = 0.5
EPSILON = 1e-06
GROUP = 4
RADIX = 1024.0
F32 = jnp.float32
BF16 = jnp.bfloat16
NT = (((1,), (1,)), ((), ()))
NN = (((1,), (0,)), ((), ()))


def halves(value):
    high = value.astype(BF16)
    return high, (value - high.astype(F32)).astype(BF16)


def dot(a, b, dims):
    return lax.dot_general(a, b, dims, preferred_element_type=F32)


def dot3(a, b_high, b_low):
    a_high, a_low = halves(a)
    return dot(a_high, b_high, NN) + dot(a_high, b_low, NN) + dot(a_low, b_high, NN)


def pair_scores(v_high, v_low, y_both):
    wide = dot(v_high, y_both, NT)
    return wide[:, :BLOCK] + wide[:, BLOCK:] + dot(v_low, y_both[:BLOCK], NT)


def pair_pull(weights, y_both):
    high, low = halves(weights)
    return dot(jnp.concatenate([high, high], axis=1), y_both, NN) + dot(low, y_both[:BLOCK], NN)


def decode(code):
    counts = jnp.floor(code * (1.0 / RADIX))
    return counts * CONFIDENCE_SCALE, code - counts * RADIX


def row_dot(a, b):
    return jnp.sum(a * b, axis=1, keepdims=True)


def build_kernel(tiles, rows, picked_ref, code_ref, entry_ref, list_ref, total_ref, dense_ref, index, buf, sem):
    slots = picked_ref.shape[0]

    def scan(i, n):
        index[n] = i
        list_ref[n] = code_ref[i]
        return n + picked_ref[i]

    total = lax.fori_loop(0, slots, scan, jnp.int32(0), unroll=8)
    total_ref[0] = total
    for extra in range(GROUP - 1):

        @pl.when(total + extra < slots)
        def _():
            index[total + extra] = 0
            list_ref[total + extra] = 0

    chunks = (total + (GROUP - 1)) // GROUP
    ids = lax.broadcasted_iota(jnp.int32, (BLOCK, entry_ref.shape[1]), 0)

    def out_copy(j, slot):
        return pltpu.make_async_copy(buf.at[slot], dense_ref.at[pl.ds(j * GROUP, GROUP)], sem.at[slot])

    def step(j, carry):
        slot = j % 2

        @pl.when(j >= 2)
        def _():
            out_copy(j - 2, slot).wait()

        for u in range(GROUP):
            place = j * GROUP + u
            which = index[place]
            base = (which // tiles) * rows + which % tiles
            users = entry_ref[pl.ds(base, 1), :]
            items = entry_ref[pl.ds(base + tiles, 1), :]
            counts = entry_ref[pl.ds(base + 2 * tiles, 1), :].astype(F32)
            user_hot = jnp.where(ids == users, 1.0, 0.0).astype(BF16)
            hit = ids == items
            item_hot = jnp.where(hit, 1.0, 0.0).astype(BF16)
            count_hot = jnp.where(hit, counts, 0.0).astype(BF16)
            both = dot(user_hot, jnp.concatenate([item_hot, count_hot], axis=0), NT)
            live = jnp.where(place < total, 1.0, 0.0)
            buf[slot, u] = (both[:, :BLOCK] + both[:, BLOCK:] * RADIX) * live
        out_copy(j, slot).start()
        return carry

    lax.fori_loop(0, chunks, step, 0)

    @pl.when(chunks >= 2)
    def _():
        out_copy(chunks - 2, chunks % 2).wait()

    @pl.when(chunks >= 1)
    def _():
        out_copy(chunks - 1, (chunks - 1) % 2).wait()


def start_kernel(grid_rows, grid_z, blocks, list_ref, total_ref, start_ref, gram_ref, dense_ref, *rest):
    owners = grid_rows * grid_z
    items = rest[:owners]
    out_ref, pair_ref = rest[owners : owners + 2]
    dense, raw, both, v_high, v_low, sem_d, sem_y, sem_o = rest[owners + 2 :]
    chunks = (total_ref[0] + (GROUP - 1)) // GROUP

    def dense_copy(j, slot):
        return pltpu.make_async_copy(dense_ref.at[pl.ds(j * GROUP, GROUP)], dense.at[slot], sem_d.at[slot])

    def pair_copy(j, slot):
        return pltpu.make_async_copy(both.at[slot], pair_ref.at[pl.ds(j * GROUP, GROUP)], sem_o.at[slot])

    def item_copy(owner, block, slot, u):
        return pltpu.make_async_copy(
            items[owner].at[pl.ds(block * BLOCK, BLOCK)], raw.at[slot, u], sem_y.at[slot, u]
        )

    def fetch(j, slot):
        dense_copy(j, slot).start()
        for u in range(GROUP):
            where = list_ref[j * GROUP + u] % 65536
            block = where % blocks
            owner = where // blocks
            for r in range(grid_rows):

                @pl.when(owner // grid_z == r)
                def _():
                    for z in range(grid_z):

                        @pl.when(owner % grid_z == z)
                        def _():
                            item_copy(r * grid_z + z, block, slot, u).start()

    @pl.when(chunks > 0)
    def _():
        fetch(0, 0)

    start = start_ref[...]
    high, low = halves(start)
    v_high[...] = high.reshape(v_high.shape)
    v_low[...] = low.reshape(v_low.shape)
    gram_high, gram_low = halves(gram_ref[...])
    out_ref[...] = -dot3(start, gram_high, gram_low).reshape(out_ref.shape)

    def step(j, carry):
        slot = j % 2

        @pl.when(j + 1 < chunks)
        def _():
            fetch(j + 1, 1 - slot)

        @pl.when(j >= 2)
        def _():
            pair_copy(j - 2, slot).wait()

        dense_copy(j, slot).wait()
        pulled = []
        for u in range(GROUP):
            item_copy(0, 0, slot, u).wait()
            block = list_ref[j * GROUP + u] // 65536
            y_high, y_low = halves(raw[slot, u])
            y_both = jnp.concatenate([y_high, y_low], axis=0)
            both[slot, u] = y_both
            fit, ones = decode(dense[slot, u])
            scores = pair_scores(v_high[block], v_low[block], y_both)
            pulled.append((block, pair_pull(ones + fit * (1.0 - scores), y_both)))
        for block, value in pulled:
            out_ref[block] += value
        pair_copy(j, slot).start()
        return carry

    lax.fori_loop(0, chunks, step, 0)

    @pl.when(chunks >= 2)
    def _():
        pair_copy(chunks - 2, chunks % 2).wait()

    @pl.when(chunks >= 1)
    def _():
        pair_copy(chunks - 1, (chunks - 1) % 2).wait()


def as_row(column, eye):
    return jnp.sum(jnp.where(eye, column, 0.0), axis=0, keepdims=True)


def as_column(row, eye):
    return jnp.sum(jnp.where(eye, row, 0.0), axis=1, keepdims=True)


def eye_mask():
    return lax.broadcasted_iota(jnp.int32, (BLOCK, BLOCK), 0) == lax.broadcasted_iota(
        jnp.int32, (BLOCK, BLOCK), 1
    )


def step_kernel(first, last, list_ref, total_ref, gram_ref, own_ref, other_ref, dense_ref, pair_ref, *rest):
    given = 1 if first else 3
    states = rest[:given]
    made = 2 if first else 4
    outs = rest[given : given + made]
    dense, both, v_high, v_low, acc, sem_d, sem_y = rest[given + made :]
    chunks = (total_ref[0] + (GROUP - 1)) // GROUP
    shape3 = v_high.shape

    def dense_copy(j, slot):
        return pltpu.make_async_copy(dense_ref.at[pl.ds(j * GROUP, GROUP)], dense.at[slot], sem_d.at[slot])

    def pair_copy(j, slot):
        return pltpu.make_async_copy(pair_ref.at[pl.ds(j * GROUP, GROUP)], both.at[slot], sem_y.at[slot])

    def fetch(j, slot):
        dense_copy(j, slot).start()
        pair_copy(j, slot).start()

    @pl.when(chunks > 0)
    def _():
        fetch(0, 0)

    summed = own_ref[...] + other_ref[...]
    if first:
        direction = summed - RIDGE * states[0][...]
        outs[0][...] = direction
    else:
        iterate, residual, direction = (ref[...] for ref in states)
        image = summed + RIDGE * direction
        norm_now = row_dot(residual, residual)
        alpha = norm_now / (row_dot(direction, image) + EPSILON)
        iterate = iterate + alpha * direction
        residual = residual - alpha * image
        norm_next = row_dot(residual, residual)
        direction = residual + norm_next / (norm_now + EPSILON) * direction
        outs[0][...] = iterate
        outs[1][...] = direction
        if last:
            eye = eye_mask()
            norms = norm_next.reshape(shape3[0], BLOCK, 1)
            for b in range(shape3[0]):
                outs[2][b : b + 1, :] = as_row(norms[b], eye)
        else:
            outs[2][...] = residual
    high, low = halves(direction)
    v_high[...] = high.reshape(shape3)
    v_low[...] = low.reshape(shape3)
    gram_high, gram_low = halves(gram_ref[...])
    base = dot3(direction, gram_high, gram_low)
    if last:
        base = direction * base
    acc[...] = base.reshape(shape3)

    def step(j, carry):
        slot = j % 2

        @pl.when(j + 1 < chunks)
        def _():
            fetch(j + 1, 1 - slot)

        dense_copy(j, slot).wait()
        pair_copy(j, slot).wait()
        pulled = []
        for u in range(GROUP):
            block = list_ref[j * GROUP + u] // 65536
            y_both = both[slot, u]
            fit, _ = decode(dense[slot, u])
            scores = pair_scores(v_high[block], v_low[block], y_both)
            weighted = fit * scores
            pulled.append((block, weighted * scores if last else pair_pull(weighted, y_both)))
        for block, value in pulled:
            acc[block] += value
        return carry

    lax.fori_loop(0, chunks, step, 0)
    if last:
        for b in range(shape3[0]):
            outs[3][b : b + 1, :] = as_row(jnp.sum(acc[b], axis=1, keepdims=True), eye)
    else:
        outs[-1][...] = acc[...].reshape(own_ref.shape)


def finish_kernel(iterate_ref, direction_ref, norm_ref, own_ref, other_ref, out_ref):
    eye = eye_mask()
    along = own_ref[...] + other_ref[...]
    for b in range(along.shape[0]):
        rows = pl.ds(b * BLOCK, BLOCK)
        direction = direction_ref[rows, :]
        curve = as_column(along[b : b + 1, :], eye) + RIDGE * row_dot(direction, direction)
        alpha = as_column(norm_ref[b : b + 1, :], eye) / (curve + EPSILON)
        out_ref[rows, :] = iterate_ref[rows, :] + alpha * direction


def place_kernel(part, slice_rows, sources, place_ref, own_ref, *rest):
    pieces = rest[: len(sources)]
    out_ref, sems = rest[len(sources) :]
    z, x = place_ref[0], place_ref[1]
    copies = [pltpu.make_async_copy(own_ref, out_ref.at[pl.ds(z * part, part)], sems.at[0])]
    for i, (mask_z, mask_x) in enumerate(sources):
        at = (z ^ mask_z) * part + (x ^ mask_x) * slice_rows
        copies.append(
            pltpu.make_async_copy(pieces[i], out_ref.at[pl.ds(at, slice_rows)], sems.at[i + 1])
        )
    for copy in copies:
        copy.start()
    for copy in copies:
        copy.wait()


SMEM = pl.BlockSpec(memory_space=pltpu.SMEM)
VMEM = pl.BlockSpec(memory_space=pltpu.VMEM)
ANY = pl.BlockSpec(memory_space=pl.ANY)


def make_shards(n_row, n_col):
    n_x = 1 << ((n_col.bit_length() - 1) // 2)
    n_z = n_col // n_x

    def swap(value, axis, mask):
        count = n_row if axis == "row" else n_col
        return lax.ppermute(value, axis, [(i, i ^ mask) for i in range(count)])

    def hop(value, pairs):
        moves = [(a * n_x + x, b * n_x + x) for a, b in pairs for x in range(n_x)]
        return lax.ppermute(value, "col", moves)

    def gather_z(value):
        if n_z != 4:
            return [value] + [swap(value, "col", k * n_x) for k in range(1, n_z)]
        out = [(1, 0), (2, 3)]
        mid = [(1, 2), (2, 1)]
        near = swap(value, "col", n_x)
        centre = hop(value, mid)
        far_end = hop(centre, out)
        far_mid = hop(near, mid)
        last_end = hop(far_mid, out)
        return [value, near, far_end + far_mid, last_end + centre]

    def shards(
        user_factors,
        item_factors,
        fetch_list,
        tile_user,
        tile_slot,
        entry_row,
        entry_col,
        entry_count,
        tile_count,
    ):
        row = lax.axis_index("row")
        col = lax.axis_index("col")
        my_z, my_x = col // n_x, col % n_x
        user_rows = user_factors.shape[0]
        part = user_rows // n_z
        part_blocks = part // BLOCK
        blocks = item_factors.shape[0] // BLOCK
        users = tile_user[0, 0]
        slots = tile_slot[0, 0]
        tiles = users.shape[0]
        width = entry_row.shape[-1]

        fetched = fetch_list[0, 0]
        peers, cap = fetched.shape
        flat = fetched.reshape(1, -1)
        local = jnp.sum(
            jnp.where(slots[:, None] == jnp.arange(peers * cap, dtype=jnp.int32)[None, :], flat, 0), axis=1
        )
        alive = jnp.arange(tiles, dtype=jnp.int32) < tile_count[0, 0]
        named = jnp.where(alive, (slots // cap) * blocks + local, -1).astype(jnp.int32)
        facts = jnp.zeros((8, width), jnp.int32).at[0, :tiles].set(users).at[1, :tiles].set(named)
        packed = jnp.concatenate([entry_row[0, 0], entry_col[0, 0], entry_count[0, 0], facts], axis=0)
        rows = packed.shape[0]
        by_z = jnp.concatenate(gather_z(packed), axis=0)
        entries = jnp.concatenate([by_z] + [swap(by_z, "col", k) for k in range(1, n_x)], axis=0)

        facts = entries.reshape(n_col, rows, width)[:, 3 * tiles : 3 * tiles + 2, :tiles]
        tile_block = facts[:, 0].reshape(-1)
        tile_item = facts[:, 1].reshape(-1)
        owner = tile_item // blocks
        owner_row, owner_col = owner // n_col, owner % n_col
        picked = (
            (tile_item >= 0) & (owner_col % n_x == my_x) & (tile_block // part_blocks == my_z)
        ).astype(jnp.int32)
        held = (owner_row ^ row) * n_z + ((owner_col // n_x) ^ my_z)
        codes = jnp.where(
            picked == 1, (tile_block % part_blocks) * 65536 + held * blocks + tile_item % blocks, 0
        ).astype(jnp.int32)
        slots_all = n_col * tiles

        listed, total, dense = pl.pallas_call(
            lambda *refs: build_kernel(tiles, rows, *refs),
            out_shape=(
                jax.ShapeDtypeStruct((slots_all,), jnp.int32),
                jax.ShapeDtypeStruct((1,), jnp.int32),
                jax.ShapeDtypeStruct((slots_all, BLOCK, BLOCK), F32),
            ),
            in_specs=[SMEM, SMEM, VMEM],
            out_specs=(SMEM, SMEM, ANY),
            scratch_shapes=[
                pltpu.SMEM((slots_all,), jnp.int32),
                pltpu.VMEM((2, GROUP, BLOCK, BLOCK), F32),
                pltpu.SemaphoreType.DMA((2,)),
            ],
            name="build",
        )(picked, codes, entries)

        along_z = gather_z(item_factors)
        by_y = [along_z] + [[swap(v, "row", 2 * m) for v in along_z] for m in range(1, n_row // 2)]
        held_items = []
        for group in by_y:
            held_items += [group, [swap(v, "row", 1) for v in group]]
        held_items = [v for group in held_items for v in group]
        gram = sum(
            jnp.dot(v.T, v, precision=lax.Precision.HIGH, preferred_element_type=F32) for v in held_items
        )

        start = lax.dynamic_slice(user_factors, (my_z * part, 0), (part, K))
        dense_shape = (2, GROUP, BLOCK, BLOCK)
        pair_shape = (2, GROUP, 2 * BLOCK, K)
        half_shape = (part_blocks, BLOCK, K)
        terms, pairs = pl.pallas_call(
            lambda *refs: start_kernel(n_row, n_z, blocks, *refs),
            out_shape=(
                jax.ShapeDtypeStruct(half_shape, F32),
                jax.ShapeDtypeStruct((slots_all, 2 * BLOCK, K), BF16),
            ),
            in_specs=[SMEM, SMEM, VMEM, VMEM, ANY] + [ANY] * len(held_items),
            out_specs=(VMEM, ANY),
            scratch_shapes=[
                pltpu.VMEM(dense_shape, F32),
                pltpu.VMEM((2, GROUP, BLOCK, K), F32),
                pltpu.VMEM(pair_shape, BF16),
                pltpu.VMEM(half_shape, BF16),
                pltpu.VMEM(half_shape, BF16),
                pltpu.SemaphoreType.DMA((2,)),
                pltpu.SemaphoreType.DMA((2, GROUP)),
                pltpu.SemaphoreType.DMA((2,)),
            ],
            name="start",
        )(listed, total, start, gram, dense, *held_items)
        terms = terms.reshape(part, K)

        def shared(value):
            others = [swap(value, "col", k) for k in range(1, n_x)]
            if n_x == 2:
                return value, others[0]
            stacked = jnp.take(jnp.stack([value] + others), my_x ^ jnp.arange(n_x), axis=0)
            return jnp.sum(stacked, axis=0), jnp.zeros_like(value)

        vector = jax.ShapeDtypeStruct((part, K), F32)
        scalars = jax.ShapeDtypeStruct((part_blocks, BLOCK), F32)

        def advance(first, last, value, states):
            own, other = shared(value)
            outs = (vector, vector) if first else (vector, vector, scalars if last else vector)
            outs = outs if first else outs + (scalars if last else vector,)
            return pl.pallas_call(
                lambda *refs: step_kernel(first, last, *refs),
                out_shape=outs,
                in_specs=[SMEM, SMEM, VMEM, VMEM, VMEM, ANY, ANY] + [VMEM] * len(states),
                out_specs=tuple(VMEM for _ in outs),
                scratch_shapes=[
                    pltpu.VMEM(dense_shape, F32),
                    pltpu.VMEM(pair_shape, BF16),
                    pltpu.VMEM(half_shape, BF16),
                    pltpu.VMEM(half_shape, BF16),
                    pltpu.VMEM(half_shape, F32),
                    pltpu.SemaphoreType.DMA((2,)),
                    pltpu.SemaphoreType.DMA((2,)),
                ],
                name="first" if first else "last" if last else "mid",
            )(listed, total, gram, own, other, dense, pairs, *states)

        residual, terms = advance(True, False, terms, (start,))
        iterate, direction, residual, terms = advance(False, False, terms, (start, residual, residual))
        iterate, direction, norms, along = advance(False, True, terms, (iterate, residual, direction))
        own, other = shared(along)
        solved = pl.pallas_call(
            finish_kernel,
            out_shape=vector,
            in_specs=[VMEM] * 5,
            out_specs=VMEM,
            name="finish",
        )(iterate, direction, norms, own, other)

        slice_rows = part // n_x
        mine = lax.dynamic_slice(solved, (my_x * slice_rows, 0), (slice_rows, K))
        sources, pieces = [], []
        for mask_z, piece in enumerate(gather_z(mine)):
            if mask_z:
                for mask_x in range(n_x):
                    sources.append((mask_z, mask_x))
                    pieces.append(swap(piece, "col", mask_x) if mask_x else piece)
        return pl.pallas_call(
            lambda *refs: place_kernel(part, slice_rows, sources, *refs),
            out_shape=jax.ShapeDtypeStruct((user_rows, K), F32),
            in_specs=[SMEM] + [ANY] * (1 + len(pieces)),
            out_specs=ANY,
            scratch_shapes=[pltpu.SemaphoreType.DMA((1 + len(pieces),))],
            name="place",
        )(jnp.stack([my_z, my_x]).astype(jnp.int32), solved, *pieces)

    return shards


def solution(mesh):
    return jax.shard_map(
        make_shards(mesh.shape["row"], mesh.shape["col"]),
        mesh=mesh,
        in_specs=(
            P("row", None),
            P(("row", "col"), None),
            P("row", "col", None, None),
            P("row", "col", None),
            P("row", "col", None),
            P("row", "col", None, None),
            P("row", "col", None, None),
            P("row", "col", None, None),
            P("row", "col"),
        ),
        out_specs=P("row", None),
        check_vma=False,
    )
```

```python
import jax
import jax.numpy as jnp
from jax import lax
from jax.experimental import pallas as pl
from jax.experimental.pallas import tpu as pltpu
from jax.sharding import PartitionSpec as P


K = 128
BLOCK = 128
ITERS = 3
CONFIDENCE_SCALE = 40.0
RIDGE = 0.5
EPSILON = 1e-06
GROUP_BITS = 3
GROUP = 1 << GROUP_BITS
RADIX = 1024.0
F32 = jnp.float32
BF16 = jnp.bfloat16
NT = (((1,), (1,)), ((), ()))
NN = (((1,), (0,)), ((), ()))


def halves(value):
    high = value.astype(BF16)
    return high, (value - high.astype(F32)).astype(BF16)


def dot(a, b, dims):
    return lax.dot_general(a, b, dims, preferred_element_type=F32)


def dot3(a, b_high, b_low):
    a_high, a_low = halves(a)
    return dot(a_high, b_high, NN) + dot(a_high, b_low, NN) + dot(a_low, b_high, NN)


def pair_scores(v_high, v_low, y_both):
    wide = dot(v_high, y_both, NT)
    return wide[:, :BLOCK] + wide[:, BLOCK:] + dot(v_low, y_both[:BLOCK], NT)


def pair_pull(weights, y_both):
    high, low = halves(weights)
    return dot(jnp.concatenate([high, high], axis=1), y_both, NN) + dot(low, y_both[:BLOCK], NN)


def decode(code):
    counts = jnp.floor(code * (1.0 / RADIX))
    return counts * CONFIDENCE_SCALE, code - counts * RADIX


def row_dot(a, b):
    high, low = halves(a * b)
    return dot(jnp.concatenate([high, low], axis=1), jnp.ones((2 * K, K), BF16), NN)


def row_sums(value):
    high, low = halves(value)
    return dot(jnp.ones((8, 2 * K), BF16), jnp.concatenate([high, low], axis=1), NT)[:1]


def build_kernel(tiles, part_blocks, owned, sides, mine_ref, *rest):
    sources = len(rest) - 9
    given = rest[:sources]
    list_ref, total_ref, dense_ref, index, facts, entry_ref, buf, sem, sem_e = rest[sources:]
    rows = given[0].shape[0]
    fact_copies = [
        pltpu.make_async_copy(ref.at[pl.ds(3 * tiles, 8), pl.ds(0, BLOCK)], facts.at[s], sem_e.at[0, s])
        for s, ref in enumerate(given)
    ]
    entry_copies = [
        pltpu.make_async_copy(ref, entry_ref.at[pl.ds(s * rows, rows)], sem_e.at[1, s])
        for s, ref in enumerate(given)
    ]
    for copy in fact_copies + entry_copies:
        copy.start()
    for copy in fact_copies:
        copy.wait()
    my_z, my_x, flip = mine_ref[0], mine_ref[1], mine_ref[2]
    owned_bits, part_bits = owned.bit_length() - 1, part_blocks.bit_length() - 1
    side_blocks = part_blocks // sides
    side_bits = side_blocks.bit_length() - 1
    last = list_ref.shape[0] // GROUP - 1

    def spot(k, side):
        back = ((last - (k >> GROUP_BITS)) << GROUP_BITS) | (k & (GROUP - 1))
        return jnp.where(side == 1, back, k)

    totals = (jnp.int32(0), jnp.int32(0))
    for source in range(sources):

        def scan(t, n, source=source):
            user = facts[source, 0, t]
            item = facts[source, 1, t]
            side = (user >> side_bits) & (sides - 1)
            at = spot(jnp.where(side == 1, n[1], n[0]), side)
            index[at] = source * rows + t
            list_ref[at] = ((user & (side_blocks - 1)) << 16) | ((item & (owned - 1)) ^ flip)
            missed = ((item >> owned_bits) ^ my_x) | ((user >> part_bits) ^ my_z)
            hit = jnp.where(missed == 0, 1, 0).astype(jnp.int32)
            return n[0] + hit * (1 - side), n[1] + hit * side

        totals = lax.fori_loop(0, tiles, scan, totals, unroll=8)
    chunks = []
    for side in range(2):
        total_ref[side] = totals[side]
        chunks.append((totals[side] + (GROUP - 1)) >> GROUP_BITS)
        for extra in range(GROUP - 1):
            k = totals[side] + extra

            @pl.when(k < chunks[side] * GROUP)
            def _():
                at = spot(k, side)
                index[at] = 0
                list_ref[at] = 0

    for copy in entry_copies:
        copy.wait()
    ids = lax.broadcasted_iota(jnp.int32, (BLOCK, entry_ref.shape[1]), 0)

    def out_copy(chunk, slot):
        return pltpu.make_async_copy(buf.at[slot], dense_ref.at[pl.ds(chunk * GROUP, GROUP)], sem.at[slot])

    def step(j, carry):
        slot = j & 1
        front = j < chunks[0]
        chunk = jnp.where(front, j, last - (j - chunks[0]))
        left = jnp.where(front, totals[0] - j * GROUP, totals[1] - (j - chunks[0]) * GROUP)

        @pl.when(j >= 2)
        def _():
            out_copy(0, slot).wait()

        for u in range(GROUP):
            base = index[chunk * GROUP + u]
            users = entry_ref[pl.ds(base, 1), :]
            items = entry_ref[pl.ds(base + tiles, 1), :]
            counts = entry_ref[pl.ds(base + 2 * tiles, 1), :].astype(F32)
            user_hot = jnp.where(ids == users, 1.0, 0.0).astype(BF16)
            hit = ids == items
            item_hot = jnp.where(hit, 1.0, 0.0).astype(BF16)
            count_hot = jnp.where(hit, counts, 0.0).astype(BF16)
            both = dot(user_hot, jnp.concatenate([item_hot, count_hot], axis=0), NT)
            live = jnp.where(u < left, 1.0, 0.0)
            buf[slot, u] = (both[:, :BLOCK] + both[:, BLOCK:] * RADIX) * live
        out_copy(chunk, slot).start()
        return carry

    every = chunks[0] + chunks[1]
    lax.fori_loop(0, every, step, 0)

    @pl.when(every >= 2)
    def _():
        out_copy(0, every & 1).wait()

    @pl.when(every >= 1)
    def _():
        out_copy(0, (every - 1) & 1).wait()


def choose(value, low, high, act):
    if high - low == 1:
        act(low)
        return
    middle = (low + high) // 2

    @pl.when(value < middle)
    def _():
        choose(value, low, middle, act)

    @pl.when(value >= middle)
    def _():
        choose(value, middle, high, act)


def start_kernel(side, owners, blocks, list_ref, total_ref, start_ref, dense_ref, *rest):
    items = rest[:owners]
    out_ref, pair_ref = rest[owners : owners + 2]
    dense, raw, both, v_high, v_low, sem_d, sem_y, sem_o = rest[owners + 2 :]
    chunks = (total_ref[side] + (GROUP - 1)) >> GROUP_BITS
    end = list_ref.shape[0] // GROUP - 1

    def place(j):
        return end - j if side else j

    def dense_copy(j, slot):
        return pltpu.make_async_copy(dense_ref.at[pl.ds(place(j) * GROUP, GROUP)], dense.at[slot], sem_d.at[slot])

    def pair_copy(j, slot):
        return pltpu.make_async_copy(both.at[slot], pair_ref.at[pl.ds(place(j) * GROUP, GROUP)], sem_o.at[slot])

    def item_copy(owner, block, slot, u):
        return pltpu.make_async_copy(
            items[owner].at[pl.ds(block * BLOCK, BLOCK)], raw.at[slot, u], sem_y.at[slot, u]
        )

    def fetch(j, slot):
        dense_copy(j, slot).start()
        for u in range(GROUP):
            where = list_ref[place(j) * GROUP + u] & 65535
            block = where & (blocks - 1)
            owner = where >> (blocks.bit_length() - 1)
            choose(owner, 0, owners, lambda o, u=u, block=block: item_copy(o, block, slot, u).start())

    @pl.when(chunks > 0)
    def _():
        fetch(0, 0)

    high, low = halves(start_ref[...])
    v_high[...] = high.reshape(v_high.shape)
    v_low[...] = low.reshape(v_low.shape)
    out_ref[...] = jnp.zeros_like(out_ref)

    def step(j, carry):
        slot = j & 1

        @pl.when(j + 1 < chunks)
        def _():
            fetch(j + 1, 1 - slot)

        @pl.when(j >= 2)
        def _():
            pair_copy(j - 2, slot).wait()

        dense_copy(j, slot).wait()
        pulled = []
        for u in range(GROUP):
            item_copy(0, 0, slot, u).wait()
            block = list_ref[place(j) * GROUP + u] >> 16
            y_high, y_low = halves(raw[slot, u])
            y_both = jnp.concatenate([y_high, y_low], axis=0)
            both[slot, u] = y_both
            fit, ones = decode(dense[slot, u])
            scores = pair_scores(v_high[block], v_low[block], y_both)
            pulled.append((block, pair_pull(ones + fit * (1.0 - scores), y_both)))
        for block, value in pulled:
            out_ref[block] += value
        pair_copy(j, slot).start()
        return carry

    lax.fori_loop(0, chunks, step, 0)

    @pl.when(chunks >= 2)
    def _():
        pair_copy(chunks - 2, chunks & 1).wait()

    @pl.when(chunks >= 1)
    def _():
        pair_copy(chunks - 1, (chunks - 1) & 1).wait()


def as_column(row, eye):
    return jnp.sum(jnp.where(eye, row, 0.0), axis=1, keepdims=True)


def eye_mask():
    return lax.broadcasted_iota(jnp.int32, (BLOCK, BLOCK), 0) == lax.broadcasted_iota(
        jnp.int32, (BLOCK, BLOCK), 1
    )


def step_kernel(side, first, last, list_ref, total_ref, gram_ref, own_ref, other_ref, dense_ref, pair_ref, *rest):
    given = 1 if first else 3
    states = rest[:given]
    made = 2 if first else 5 if last else 4
    outs = rest[given : given + made]
    dense, both, v_high, v_low, acc, sem_d, sem_y = rest[given + made :]
    chunks = (total_ref[side] + (GROUP - 1)) >> GROUP_BITS
    end = list_ref.shape[0] // GROUP - 1

    def place(j):
        return end - j if side else j

    shape3 = v_high.shape

    def dense_copy(j, slot):
        return pltpu.make_async_copy(dense_ref.at[pl.ds(place(j) * GROUP, GROUP)], dense.at[slot], sem_d.at[slot])

    def pair_copy(j, slot):
        return pltpu.make_async_copy(pair_ref.at[pl.ds(place(j) * GROUP, GROUP)], both.at[slot], sem_y.at[slot])

    def fetch(j, slot):
        dense_copy(j, slot).start()
        pair_copy(j, slot).start()

    @pl.when(chunks > 0)
    def _():
        fetch(0, 0)

    summed = own_ref[...] + other_ref[...]
    gram_high, gram_low = halves(gram_ref[...])
    if first:
        start = states[0][...]
        direction = summed - dot3(start, gram_high, gram_low) - RIDGE * start
        outs[0][...] = direction
    else:
        iterate, residual, direction = (ref[...] for ref in states)
        image = summed + dot3(direction, gram_high, gram_low) + RIDGE * direction
        norm_now = row_dot(residual, residual)
        alpha = norm_now / (row_dot(direction, image) + EPSILON)
        iterate = iterate + alpha * direction
        residual = residual - alpha * image
        norm_next = row_dot(residual, residual)
        direction = residual + norm_next / (norm_now + EPSILON) * direction
        outs[0][...] = iterate
        outs[1][...] = direction
        if last:
            for b in range(shape3[0]):
                rows = slice(b * BLOCK, (b + 1) * BLOCK)
                outs[2][b : b + 1, :] = row_sums(residual[rows] * residual[rows])
                along = dot3(direction[rows], gram_high, gram_low) + RIDGE * direction[rows]
                outs[4][b : b + 1, :] = row_sums(direction[rows] * along)
        else:
            outs[2][...] = residual
    high, low = halves(direction)
    v_high[...] = high.reshape(shape3)
    v_low[...] = low.reshape(shape3)
    acc[...] = jnp.zeros_like(acc)

    def step(j, carry):
        slot = j & 1

        @pl.when(j + 1 < chunks)
        def _():
            fetch(j + 1, 1 - slot)

        dense_copy(j, slot).wait()
        pair_copy(j, slot).wait()
        pulled = []
        for u in range(GROUP):
            block = list_ref[place(j) * GROUP + u] >> 16
            y_both = both[slot, u]
            fit, _ = decode(dense[slot, u])
            scores = pair_scores(v_high[block], v_low[block], y_both)
            weighted = fit * scores
            pulled.append((block, weighted * scores if last else pair_pull(weighted, y_both)))
        for block, value in pulled:
            acc[block] += value
        return carry

    lax.fori_loop(0, chunks, step, 0)
    if last:
        for b in range(shape3[0]):
            outs[3][b : b + 1, :] = row_sums(acc[b])
    else:
        outs[3 if not first else 1][...] = acc[...].reshape(own_ref.shape)


def finish_kernel(slice_rows, sides, place_ref, *rest):
    out_ref, mine_ref = rest[-2:]
    eye = eye_mask()
    done = 0
    for side in range(sides):
        iterate_ref, direction_ref, norm_ref, square_ref, own_ref, other_ref = rest[6 * side : 6 * side + 6]
        curve = own_ref[...] + other_ref[...] + square_ref[...]
        alpha = norm_ref[...] / (curve + EPSILON)
        for b in range(alpha.shape[0]):
            rows = pl.ds(b * BLOCK, BLOCK)
            out_ref[pl.ds(done, BLOCK), :] = (
                iterate_ref[rows, :] + as_column(alpha[b : b + 1, :], eye) * direction_ref[rows, :]
            )
            done += BLOCK
    mine_ref[...] = out_ref[pl.ds(pl.multiple_of(place_ref[1] * slice_rows, 8), slice_rows), :]


def place_kernel(part, slice_rows, sources, place_ref, own_ref, *rest):
    pieces = rest[: len(sources)]
    out_ref = rest[-1]
    z, x = place_ref[0], place_ref[1]
    out_ref[pl.ds(pl.multiple_of(z * part, 8), part), :] = own_ref[...]
    for (mask_z, mask_x), piece in zip(sources, pieces):
        at = (z ^ mask_z) * part + (x ^ mask_x) * slice_rows
        out_ref[pl.ds(pl.multiple_of(at, 8), slice_rows), :] = piece[...]


SMEM = pl.BlockSpec(memory_space=pltpu.SMEM)
VMEM = pl.BlockSpec(memory_space=pltpu.VMEM)
ANY = pl.BlockSpec(memory_space=pl.ANY)


def make_shards(n_row, n_col):
    n_x = 1 << ((n_col.bit_length() - 1) // 2)
    n_z = n_col // n_x

    def swap(value, axis, mask):
        count = n_row if axis == "row" else n_col
        return lax.ppermute(value, axis, [(i, i ^ mask) for i in range(count)])

    def hop(value, pairs):
        return lax.ppermute(value, "col", [(a * n_x + x, b * n_x + x) for a, b in pairs for x in range(n_x)])

    def direct_z(value):
        return [value] + [swap(value, "col", k * n_x) for k in range(1, n_z)]

    def gather_z(value):
        if n_z != 4:
            return direct_z(value)
        near = swap(value, "col", n_x)
        across = swap(value, "col", 3 * n_x)
        middle = hop(near, [(1, 2), (2, 1)])
        ends = hop(across, [(1, 0), (2, 3)])
        return [value, near, middle + ends, across]

    def shards(
        user_factors,
        item_factors,
        fetch_list,
        tile_user,
        tile_slot,
        entry_row,
        entry_col,
        entry_count,
        tile_count,
    ):
        row = lax.axis_index("row")
        col = lax.axis_index("col")
        my_z, my_x = col // n_x, col % n_x
        user_rows = user_factors.shape[0]
        part = user_rows // n_z
        part_blocks = part // BLOCK
        sides = 2 if part_blocks % 2 == 0 else 1
        side_rows = part // sides
        side_blocks = part_blocks // sides
        blocks = item_factors.shape[0] // BLOCK
        users = tile_user[0, 0]
        slots = tile_slot[0, 0]
        tiles = users.shape[0]
        width = entry_row.shape[-1]

        fetched = fetch_list[0, 0]
        peers, cap = fetched.shape
        flat = fetched.reshape(1, -1)
        local = jnp.sum(
            jnp.where(slots[:, None] == jnp.arange(peers * cap, dtype=jnp.int32)[None, :], flat, 0), axis=1
        )
        alive = jnp.arange(tiles, dtype=jnp.int32) < tile_count[0, 0]
        owner = slots // cap
        owner_row, owner_z, owner_x = owner // n_col, owner % n_col // n_x, owner % n_x
        owned = n_row * n_z * blocks
        named = owner_x * owned + (owner_row * n_z + owner_z) * blocks + local
        facts = jnp.stack([users, jnp.where(alive, named, -1).astype(jnp.int32)])
        facts = jnp.pad(facts, ((0, 6), (0, width - tiles)))
        packed = jnp.concatenate([entry_row[0, 0], entry_col[0, 0], entry_count[0, 0], facts], axis=0)
        entries = direct_z(packed)
        entries += [swap(v, "col", k) for k in range(1, n_x) for v in entries]
        slots_all = n_col * tiles + GROUP
        place = jnp.stack([my_z, my_x, (row * n_z + my_z) * blocks]).astype(jnp.int32)

        listed, total, dense = pl.pallas_call(
            lambda *refs: build_kernel(tiles, part_blocks, owned, sides, *refs),
            out_shape=(
                jax.ShapeDtypeStruct((slots_all,), jnp.int32),
                jax.ShapeDtypeStruct((2,), jnp.int32),
                jax.ShapeDtypeStruct((slots_all, BLOCK, BLOCK), F32),
            ),
            in_specs=[SMEM] + [ANY] * n_col,
            out_specs=(SMEM, SMEM, ANY),
            scratch_shapes=[
                pltpu.SMEM((slots_all,), jnp.int32),
                pltpu.SMEM((n_col, 8, BLOCK), jnp.int32),
                pltpu.VMEM((n_col * packed.shape[0], width), jnp.int32),
                pltpu.VMEM((2, GROUP, BLOCK, BLOCK), F32),
                pltpu.SemaphoreType.DMA((2,)),
                pltpu.SemaphoreType.DMA((2, n_col)),
            ],
            name="build",
        )(place, *entries)

        along_z = gather_z(item_factors)
        by_y = [along_z]
        for m in range(1, n_row // 2):
            by_y.append([swap(v, "row", 2 * m) for v in along_z])
        held_items = []
        for group in by_y:
            held_items += [group, [swap(v, "row", 1) for v in group]]
        held_items = [v for group in held_items for v in group]
        gram = jnp.dot(
            item_factors.T, item_factors, precision=lax.Precision.HIGH, preferred_element_type=F32
        )
        for axis, count, mask in (("col", n_x, 1), ("row", n_row, 1), ("col", n_col, n_x)):
            while mask < count:
                gram = gram + swap(gram, axis, mask)
                mask *= 2

        dense_shape = (2, GROUP, BLOCK, BLOCK)
        pair_shape = (2, GROUP, 2 * BLOCK, K)
        half_shape = (side_blocks, BLOCK, K)

        def begin(side):
            start = lax.dynamic_slice(user_factors, (my_z * part + side * side_rows, 0), (side_rows, K))
            terms, pairs = pl.pallas_call(
                lambda *refs: start_kernel(side, n_row * n_z, blocks, *refs),
                out_shape=(
                    jax.ShapeDtypeStruct(half_shape, F32),
                    jax.ShapeDtypeStruct((slots_all, 2 * BLOCK, K), BF16),
                ),
                in_specs=[SMEM, SMEM, VMEM, ANY] + [ANY] * len(held_items),
                out_specs=(VMEM, ANY),
                scratch_shapes=[
                    pltpu.VMEM(dense_shape, F32),
                    pltpu.VMEM((2, GROUP, BLOCK, K), F32),
                    pltpu.VMEM(pair_shape, BF16),
                    pltpu.VMEM(half_shape, BF16),
                    pltpu.VMEM(half_shape, BF16),
                    pltpu.SemaphoreType.DMA((2,)),
                    pltpu.SemaphoreType.DMA((2, GROUP)),
                    pltpu.SemaphoreType.DMA((2,)),
                ],
            )(listed, total, start, dense, *held_items)
            return start, terms.reshape(side_rows, K), pairs

        def shared(value):
            others = [swap(value, "col", k) for k in range(1, n_x)]
            if n_x == 2:
                return value, others[0]
            stacked = jnp.take(jnp.stack([value] + others), my_x ^ jnp.arange(n_x), axis=0)
            return jnp.sum(stacked, axis=0), jnp.zeros_like(value)

        vector = jax.ShapeDtypeStruct((side_rows, K), F32)
        scalars = jax.ShapeDtypeStruct((side_blocks, BLOCK), F32)

        def advance(side, count, value, pairs, states):
            first, last = count == 0, count == ITERS - 1
            own, other = shared(value)
            outs = (vector, vector) if first else (vector, vector, scalars if last else vector)
            outs = outs if first else outs + ((scalars, scalars) if last else (vector,))
            return pl.pallas_call(
                lambda *refs: step_kernel(side, first, last, *refs),
                out_shape=outs,
                in_specs=[SMEM, SMEM, VMEM, VMEM, VMEM, ANY, ANY] + [VMEM] * len(states),
                out_specs=tuple(VMEM for _ in outs),
                scratch_shapes=[
                    pltpu.VMEM(dense_shape, F32),
                    pltpu.VMEM(pair_shape, BF16),
                    pltpu.VMEM(half_shape, BF16),
                    pltpu.VMEM(half_shape, BF16),
                    pltpu.VMEM(half_shape, F32),
                    pltpu.SemaphoreType.DMA((2,)),
                    pltpu.SemaphoreType.DMA((2,)),
                ],
            )(listed, total, gram, own, other, dense, pairs, *states)

        started = [begin(side) for side in range(sides)]
        states = [(start,) for start, _, _ in started]
        values = [terms for _, terms, _ in started]
        for count in range(ITERS):
            for side in range(sides):
                results = advance(side, count, values[side], started[side][2], states[side])
                if count == ITERS - 1:
                    iterate, direction, norms, values[side], squares = results
                    states[side] = (iterate, direction, norms, squares)
                elif count:
                    iterate, direction, residual, values[side] = results
                    states[side] = (iterate, residual, direction)
                else:
                    residual, values[side] = results
                    states[side] = (states[side][0], residual, residual)
        inputs = []
        for side in range(sides):
            inputs += [*states[side], *shared(values[side])]
        slice_rows = part // n_x
        solved, mine = pl.pallas_call(
            lambda *refs: finish_kernel(slice_rows, sides, *refs),
            out_shape=(jax.ShapeDtypeStruct((part, K), F32), jax.ShapeDtypeStruct((slice_rows, K), F32)),
            in_specs=[SMEM] + [VMEM] * len(inputs),
            out_specs=(VMEM, VMEM),
            name="finish",
        )(place, *inputs)

        sources, pieces = [], []
        for mask_z, piece in enumerate(direct_z(mine)):
            if mask_z:
                for mask_x in range(n_x):
                    sources.append((mask_z, mask_x))
                    pieces.append(swap(piece, "col", mask_x) if mask_x else piece)
        return pl.pallas_call(
            lambda *refs: place_kernel(part, slice_rows, sources, *refs),
            out_shape=jax.ShapeDtypeStruct((user_rows, K), F32),
            in_specs=[SMEM] + [VMEM] * (1 + len(pieces)),
            out_specs=VMEM,
            name="place",
        )(place, solved, *pieces)

    return shards


def solution(mesh):
    n_row, n_col = mesh.shape["row"], mesh.shape["col"]
    inner = make_shards(n_row, n_col)

    return jax.shard_map(
        inner,
        mesh=mesh,
        in_specs=(
            P("row", None),
            P(("row", "col"), None),
            P("row", "col", None, None),
            P("row", "col", None),
            P("row", "col", None),
            P("row", "col", None, None),
            P("row", "col", None, None),
            P("row", "col", None, None),
            P("row", "col"),
        ),
        out_specs=P("row", None),
        check_vma=False,
    )
```

```python
import jax
import jax.numpy as jnp
from jax import lax
from jax.experimental import pallas as pl
from jax.experimental.pallas import tpu as pltpu
from jax.sharding import PartitionSpec as P


K = 128
BLOCK = 128
ITERS = 3
CONFIDENCE_SCALE = 40.0
RIDGE = 0.5
EPSILON = 1e-06
GROUP_BITS = 3
GROUP = 1 << GROUP_BITS
RADIX = 1024.0
F32 = jnp.float32
BF16 = jnp.bfloat16
NT = (((1,), (1,)), ((), ()))
NN = (((1,), (0,)), ((), ()))


def halves(value):
    high = value.astype(BF16)
    return high, (value - high.astype(F32)).astype(BF16)


def dot(a, b, dims):
    return lax.dot_general(a, b, dims, preferred_element_type=F32)


def dot3(a, b_high, b_low):
    a_high, a_low = halves(a)
    return dot(a_high, b_high, NN) + dot(a_high, b_low, NN) + dot(a_low, b_high, NN)


def pair_scores(v_high, v_low, y_both):
    wide = dot(v_high, y_both, NT)
    return wide[:, :BLOCK] + wide[:, BLOCK:] + dot(v_low, y_both[:BLOCK], NT)


def pair_pull(weights, y_both):
    high, low = halves(weights)
    return dot(jnp.concatenate([high, high], axis=1), y_both, NN) + dot(low, y_both[:BLOCK], NN)


def decode(code):
    counts = jnp.floor(code * (1.0 / RADIX))
    return counts * CONFIDENCE_SCALE, code - counts * RADIX


def row_dot(a, b):
    high, low = halves(a * b)
    return dot(jnp.concatenate([high, low], axis=1), jnp.ones((2 * K, K), BF16), NN)


def row_sums(value):
    high, low = halves(value)
    return dot(jnp.ones((8, 2 * K), BF16), jnp.concatenate([high, low], axis=1), NT)[:1]


def build_kernel(tiles, part_blocks, owned, sides, mine_ref, *rest):
    sources = len(rest) - 9
    given = rest[:sources]
    list_ref, total_ref, dense_ref, index, facts, entry_ref, buf, sem, sem_e = rest[sources:]
    rows = given[0].shape[0]
    fact_copies = [
        pltpu.make_async_copy(ref.at[pl.ds(3 * tiles, 8), pl.ds(0, BLOCK)], facts.at[s], sem_e.at[0, s])
        for s, ref in enumerate(given)
    ]
    entry_copies = [
        pltpu.make_async_copy(ref, entry_ref.at[pl.ds(s * rows, rows)], sem_e.at[1, s])
        for s, ref in enumerate(given)
    ]
    for copy in fact_copies + entry_copies:
        copy.start()
    for copy in fact_copies:
        copy.wait()
    my_z, my_x, flip = mine_ref[0], mine_ref[1], mine_ref[2]
    owned_bits, part_bits = owned.bit_length() - 1, part_blocks.bit_length() - 1
    side_blocks = part_blocks // sides
    side_bits = side_blocks.bit_length() - 1
    last = list_ref.shape[0] // GROUP - 1

    def spot(k, side):
        back = ((last - (k >> GROUP_BITS)) << GROUP_BITS) | (k & (GROUP - 1))
        return jnp.where(side == 1, back, k)

    totals = (jnp.int32(0), jnp.int32(0))
    for source in range(sources):

        def scan(t, n, source=source):
            user = facts[source, 0, t]
            item = facts[source, 1, t]
            side = (user >> side_bits) & (sides - 1)
            at = spot(jnp.where(side == 1, n[1], n[0]), side)
            index[at] = source * rows + t
            list_ref[at] = ((user & (side_blocks - 1)) << 16) | ((item & (owned - 1)) ^ flip)
            missed = ((item >> owned_bits) ^ my_x) | ((user >> part_bits) ^ my_z)
            hit = jnp.where(missed == 0, 1, 0).astype(jnp.int32)
            return n[0] + hit * (1 - side), n[1] + hit * side

        totals = lax.fori_loop(0, tiles, scan, totals, unroll=8)
    chunks = []
    for side in range(2):
        total_ref[side] = totals[side]
        chunks.append((totals[side] + (GROUP - 1)) >> GROUP_BITS)
        for extra in range(GROUP - 1):
            k = totals[side] + extra

            @pl.when(k < chunks[side] * GROUP)
            def _():
                at = spot(k, side)
                index[at] = 0
                list_ref[at] = 0

    for copy in entry_copies:
        copy.wait()
    ids = lax.broadcasted_iota(jnp.int32, (BLOCK, entry_ref.shape[1]), 0)

    def out_copy(chunk, slot):
        return pltpu.make_async_copy(buf.at[slot], own_chunk(dense_ref, chunk), sem.at[slot])

    def step(j, carry):
        slot = j & 1
        front = j < chunks[0]
        chunk = jnp.where(front, j, last - (j - chunks[0]))
        left = jnp.where(front, totals[0] - j * GROUP, totals[1] - (j - chunks[0]) * GROUP)

        @pl.when(j >= 2)
        def _():
            out_copy(0, slot).wait()

        for u in range(GROUP):
            base = index[chunk * GROUP + u]
            users = entry_ref[pl.ds(base, 1), :]
            items = entry_ref[pl.ds(base + tiles, 1), :]
            counts = entry_ref[pl.ds(base + 2 * tiles, 1), :].astype(F32)
            user_hot = jnp.where(ids == users, 1.0, 0.0).astype(BF16)
            hit = ids == items
            item_hot = jnp.where(hit, 1.0, 0.0).astype(BF16)
            count_hot = jnp.where(hit, counts, 0.0).astype(BF16)
            both = dot(user_hot, jnp.concatenate([item_hot, count_hot], axis=0), NT)
            live = jnp.where(u < left, 1.0, 0.0)
            buf[slot, u] = (both[:, :BLOCK] + both[:, BLOCK:] * RADIX) * live
        out_copy(chunk, slot).start()
        return carry

    every = chunks[0] + chunks[1]
    lax.fori_loop(0, every, step, 0)

    @pl.when(every >= 2)
    def _():
        out_copy(0, every & 1).wait()

    @pl.when(every >= 1)
    def _():
        out_copy(0, (every - 1) & 1).wait()


def own_chunk(ref, chunk):
    return ref.at[pl.ds(chunk * GROUP, GROUP)]


def read_chunk(ref, chunk, scratch):
    if not scratch:
        return own_chunk(ref, chunk)
    pltpu.sync_copy(own_chunk(ref, chunk), scratch[0])
    return scratch[0]


def near(value):
    return pltpu.with_memory_space_constraint(value, pltpu.VMEM)


def far(value):
    return pltpu.with_memory_space_constraint(value, pltpu.HBM)


def choose(value, low, high, act):
    if high - low == 1:
        act(low)
        return
    middle = (low + high) // 2

    @pl.when(value < middle)
    def _():
        choose(value, low, middle, act)

    @pl.when(value >= middle)
    def _():
        choose(value, middle, high, act)


def bring_kernel(list_ref, total_ref, dense_ref, kept_ref, sem):
    chunks = [(total_ref[side] + (GROUP - 1)) >> GROUP_BITS for side in range(2)]

    def dense_copy(j):
        chunk = jnp.where(j < chunks[0], j, list_ref.shape[0] // GROUP - 1 - (j - chunks[0]))
        return pltpu.make_async_copy(own_chunk(dense_ref, chunk), own_chunk(kept_ref, chunk), sem.at[j])

    def begin(j, carry):
        dense_copy(j).start()
        return carry

    def end(j, carry):
        dense_copy(j).wait()
        return carry

    lax.fori_loop(0, chunks[0] + chunks[1], begin, 0)
    lax.fori_loop(0, chunks[0] + chunks[1], end, 0)


def gather_kernel(owners, blocks, list_ref, total_ref, *rest):
    items = rest[:owners]
    pair_ref = rest[owners]
    buf = rest[owners + 1 :]
    front, back = (((total_ref[side] + (GROUP - 1)) >> GROUP_BITS) << GROUP_BITS for side in range(2))
    slots = list_ref.shape[0]

    def step(j, carry):
        at = jnp.where(j < front, j, slots - back + (j - front))
        where = list_ref[at] & 65535
        rows = pl.ds(pl.multiple_of((where & (blocks - 1)) * BLOCK, BLOCK), BLOCK)
        target = buf[0] if buf else pair_ref.at[at]

        def split(owner):
            high, low = halves(items[owner][rows, :])
            target[:BLOCK, :] = high
            target[BLOCK:, :] = low

        choose(where >> (blocks.bit_length() - 1), 0, owners, split)
        if buf:
            pltpu.sync_copy(target, pair_ref.at[at])
        return carry

    lax.fori_loop(0, front + back, step, 0)


def start_kernel(side, list_ref, total_ref, start_ref, dense_ref, pair_ref, out_ref, v_high, v_low, *copies):
    chunks = (total_ref[side] + (GROUP - 1)) >> GROUP_BITS
    end = list_ref.shape[0] // GROUP - 1
    high, low = halves(start_ref[...])
    v_high[...] = high.reshape(v_high.shape)
    v_low[...] = low.reshape(v_low.shape)
    out_ref[...] = jnp.zeros_like(out_ref)

    def step(j, carry):
        chunk = end - j if side else j
        dense = read_chunk(dense_ref, chunk, copies[:1])
        both = read_chunk(pair_ref, chunk, copies[1:])
        pulled = []
        for u in range(GROUP):
            block = list_ref[chunk * GROUP + u] >> 16
            y_both = both[u]
            fit, ones = decode(dense[u])
            scores = pair_scores(v_high[block], v_low[block], y_both)
            pulled.append((block, pair_pull(ones + fit * (1.0 - scores), y_both)))
        for block, value in pulled:
            out_ref[block] += value
        return carry

    lax.fori_loop(0, chunks, step, 0)


def as_column(row, eye):
    return jnp.sum(jnp.where(eye, row, 0.0), axis=1, keepdims=True)


def eye_mask():
    return lax.broadcasted_iota(jnp.int32, (BLOCK, BLOCK), 0) == lax.broadcasted_iota(
        jnp.int32, (BLOCK, BLOCK), 1
    )


def step_kernel(side, first, last, list_ref, total_ref, gram_ref, own_ref, other_ref, dense_ref, pair_ref, *rest):
    given = 1 if first else 3
    states = rest[:given]
    made = 2 if first else 5 if last else 4
    outs = rest[given : given + made]
    v_high, v_low, acc, *copies = rest[given + made :]
    shape3 = v_high.shape
    chunks = (total_ref[side] + (GROUP - 1)) >> GROUP_BITS
    end = list_ref.shape[0] // GROUP - 1
    summed = own_ref[...] + other_ref[...]
    gram_high, gram_low = halves(gram_ref[...])
    if first:
        start = states[0][...]
        direction = summed - dot3(start, gram_high, gram_low) - RIDGE * start
        outs[0][...] = direction
    else:
        iterate, residual, direction = (ref[...] for ref in states)
        image = summed + dot3(direction, gram_high, gram_low) + RIDGE * direction
        norm_now = row_dot(residual, residual)
        alpha = norm_now / (row_dot(direction, image) + EPSILON)
        iterate = iterate + alpha * direction
        residual = residual - alpha * image
        norm_next = row_dot(residual, residual)
        direction = residual + norm_next / (norm_now + EPSILON) * direction
        outs[0][...] = iterate
        outs[1][...] = direction
        if last:
            for b in range(shape3[0]):
                rows = slice(b * BLOCK, (b + 1) * BLOCK)
                outs[2][b : b + 1, :] = row_sums(residual[rows] * residual[rows])
                along = dot3(direction[rows], gram_high, gram_low) + RIDGE * direction[rows]
                outs[4][b : b + 1, :] = row_sums(direction[rows] * along)
        else:
            outs[2][...] = residual
    high, low = halves(direction)
    v_high[...] = high.reshape(shape3)
    v_low[...] = low.reshape(shape3)
    acc[...] = jnp.zeros_like(acc)

    def step(j, carry):
        chunk = end - j if side else j
        dense = read_chunk(dense_ref, chunk, copies[:1])
        both = read_chunk(pair_ref, chunk, copies[1:])
        pulled = []
        for u in range(GROUP):
            block = list_ref[chunk * GROUP + u] >> 16
            y_both = both[u]
            fit, _ = decode(dense[u])
            scores = pair_scores(v_high[block], v_low[block], y_both)
            weighted = fit * scores
            pulled.append((block, weighted * scores if last else pair_pull(weighted, y_both)))
        for block, value in pulled:
            acc[block] += value
        return carry

    lax.fori_loop(0, chunks, step, 0)
    if last:
        for b in range(shape3[0]):
            outs[3][b : b + 1, :] = row_sums(acc[b])
    else:
        outs[3 if not first else 1][...] = acc[...].reshape(own_ref.shape)


def finish_kernel(slice_rows, sides, place_ref, *rest):
    out_ref, mine_ref = rest[-2:]
    eye = eye_mask()
    done = 0
    for side in range(sides):
        iterate_ref, direction_ref, norm_ref, square_ref, own_ref, other_ref = rest[6 * side : 6 * side + 6]
        curve = own_ref[...] + other_ref[...] + square_ref[...]
        alpha = norm_ref[...] / (curve + EPSILON)
        for b in range(alpha.shape[0]):
            rows = pl.ds(b * BLOCK, BLOCK)
            out_ref[pl.ds(done, BLOCK), :] = (
                iterate_ref[rows, :] + as_column(alpha[b : b + 1, :], eye) * direction_ref[rows, :]
            )
            done += BLOCK
    mine_ref[...] = out_ref[pl.ds(pl.multiple_of(place_ref[1] * slice_rows, 8), slice_rows), :]


def place_kernel(part, slice_rows, sources, place_ref, own_ref, *rest):
    pieces = rest[: len(sources)]
    out_ref = rest[-1]
    z, x = place_ref[0], place_ref[1]
    out_ref[pl.ds(pl.multiple_of(z * part, 8), part), :] = own_ref[...]
    for (mask_z, mask_x), piece in zip(sources, pieces):
        at = (z ^ mask_z) * part + (x ^ mask_x) * slice_rows
        out_ref[pl.ds(pl.multiple_of(at, 8), slice_rows), :] = piece[...]


SMEM = pl.BlockSpec(memory_space=pltpu.SMEM)
VMEM = pl.BlockSpec(memory_space=pltpu.VMEM)
ANY = pl.BlockSpec(memory_space=pl.ANY)


def make_shards(n_row, n_col):
    n_x = 1 << ((n_col.bit_length() - 1) // 2)
    n_z = n_col // n_x

    def swap(value, axis, mask):
        count = n_row if axis == "row" else n_col
        return lax.ppermute(value, axis, [(i, i ^ mask) for i in range(count)])

    def hop(value, pairs):
        return lax.ppermute(value, "col", [(a * n_x + x, b * n_x + x) for a, b in pairs for x in range(n_x)])

    def direct_z(value):
        return [value] + [swap(value, "col", k * n_x) for k in range(1, n_z)]

    def gather_z(value):
        if n_z != 4:
            return direct_z(value)
        near = swap(value, "col", n_x)
        across = swap(value, "col", 3 * n_x)
        middle = hop(near, [(1, 2), (2, 1)])
        ends = hop(across, [(1, 0), (2, 3)])
        return [value, near, middle + ends, across]

    def shards(
        user_factors,
        item_factors,
        fetch_list,
        tile_user,
        tile_slot,
        entry_row,
        entry_col,
        entry_count,
        tile_count,
    ):
        row = lax.axis_index("row")
        col = lax.axis_index("col")
        my_z, my_x = col // n_x, col % n_x
        user_rows = user_factors.shape[0]
        part = user_rows // n_z
        part_blocks = part // BLOCK
        sides = 2 if part_blocks % 2 == 0 else 1
        side_rows = part // sides
        side_blocks = part_blocks // sides
        blocks = item_factors.shape[0] // BLOCK
        users = tile_user[0, 0]
        slots = tile_slot[0, 0]
        tiles = users.shape[0]
        width = entry_row.shape[-1]

        fetched = fetch_list[0, 0]
        peers, cap = fetched.shape
        flat = fetched.reshape(1, -1)
        local = jnp.sum(
            jnp.where(slots[:, None] == jnp.arange(peers * cap, dtype=jnp.int32)[None, :], flat, 0), axis=1
        )
        alive = jnp.arange(tiles, dtype=jnp.int32) < tile_count[0, 0]
        owner = slots // cap
        owner_row, owner_z, owner_x = owner // n_col, owner % n_col // n_x, owner % n_x
        owned = n_row * n_z * blocks
        named = owner_x * owned + (owner_row * n_z + owner_z) * blocks + local
        facts = jnp.stack([users, jnp.where(alive, named, -1).astype(jnp.int32)])
        facts = jnp.pad(facts, ((0, 6), (0, width - tiles)))
        packed = jnp.concatenate([entry_row[0, 0], entry_col[0, 0], entry_count[0, 0], facts], axis=0)
        entries = gather_z(packed)
        entries += [swap(v, "col", k) for k in range(1, n_x) for v in entries]
        slots_all = n_col * tiles + GROUP
        resident = slots_all * BLOCK * K * 8 <= 40 << 20
        limit = pltpu.CompilerParams(vmem_limit_bytes=(8 if resident else 24) << 20)
        hold, keep = (pltpu.VMEM, near) if resident else (pltpu.HBM, far)
        wide = VMEM if resident else ANY
        copied = [] if resident else [pltpu.VMEM((GROUP, BLOCK, BLOCK), F32), pltpu.VMEM((GROUP, 2 * BLOCK, K), BF16)]
        place = jnp.stack([my_z, my_x, (row * n_z + my_z) * blocks]).astype(jnp.int32)

        listed, total, dense = pl.pallas_call(
            lambda *refs: build_kernel(tiles, part_blocks, owned, sides, *refs),
            out_shape=(
                jax.ShapeDtypeStruct((slots_all,), jnp.int32),
                jax.ShapeDtypeStruct((2,), jnp.int32),
                pltpu.HBM((slots_all, BLOCK, BLOCK), F32),
            ),
            in_specs=[SMEM] + [ANY] * n_col,
            out_specs=(SMEM, SMEM, ANY),
            scratch_shapes=[
                pltpu.SMEM((slots_all,), jnp.int32),
                pltpu.SMEM((n_col, 8, BLOCK), jnp.int32),
                pltpu.VMEM((n_col * packed.shape[0], width), jnp.int32),
                pltpu.VMEM((2, GROUP, BLOCK, BLOCK), F32),
                pltpu.SemaphoreType.DMA((2,)),
                pltpu.SemaphoreType.DMA((2, n_col)),
            ],
            compiler_params=limit,
            name="build",
        )(place, *entries)

        along_z = gather_z(item_factors)
        by_y = [along_z]
        for m in range(1, n_row // 2):
            by_y.append([swap(v, "row", 2 * m) for v in along_z])
        held_items = []
        for group in by_y:
            held_items += [group, [swap(v, "row", 1) for v in group]]
        held_items = [v for group in held_items for v in group]
        gram = jnp.dot(
            item_factors.T, item_factors, precision=lax.Precision.HIGH, preferred_element_type=F32
        )
        for axis, count, mask in (("col", n_x, 1), ("row", n_row, 1), ("col", n_col, n_x)):
            while mask < count:
                gram = gram + swap(gram, axis, mask)
                mask *= 2

        if resident:
            dense = pl.pallas_call(
                bring_kernel,
                out_shape=pltpu.VMEM((slots_all, BLOCK, BLOCK), F32),
                in_specs=[SMEM, SMEM, ANY],
                out_specs=VMEM,
                scratch_shapes=[pltpu.SemaphoreType.DMA((slots_all // GROUP,))],
                compiler_params=limit,
                name="bring",
            )(listed, total, far(dense))
        pairs = pl.pallas_call(
            lambda *refs: gather_kernel(n_row * n_z, blocks, *refs),
            out_shape=hold((slots_all, 2 * BLOCK, K), BF16),
            in_specs=[SMEM, SMEM] + [VMEM] * len(held_items),
            out_specs=wide,
            scratch_shapes=[] if resident else [pltpu.VMEM((2 * BLOCK, K), BF16)],
            compiler_params=limit,
            name="gather",
        )(listed, total, *(near(v) for v in held_items))
        half_shape = (side_blocks, BLOCK, K)

        def begin(side):
            start = lax.dynamic_slice(user_factors, (my_z * part + side * side_rows, 0), (side_rows, K))
            terms = pl.pallas_call(
                lambda *refs: start_kernel(side, *refs),
                out_shape=pltpu.VMEM(half_shape, F32),
                in_specs=[SMEM, SMEM, VMEM, wide, wide],
                out_specs=VMEM,
                scratch_shapes=[pltpu.VMEM(half_shape, BF16), pltpu.VMEM(half_shape, BF16)] + copied,
                compiler_params=limit,
            )(listed, total, near(start), keep(dense), keep(pairs))
            return start, terms.reshape(side_rows, K)

        def shared(value):
            others = [swap(value, "col", k) for k in range(1, n_x)]
            if n_x == 2:
                return value, others[0]
            stacked = jnp.take(jnp.stack([value] + others), my_x ^ jnp.arange(n_x), axis=0)
            return jnp.sum(stacked, axis=0), jnp.zeros_like(value)

        vector = pltpu.VMEM((side_rows, K), F32)
        scalars = pltpu.VMEM((side_blocks, BLOCK), F32)

        def advance(side, count, value, states):
            first, last = count == 0, count == ITERS - 1
            own, other = shared(value)
            outs = (vector, vector) if first else (vector, vector, scalars if last else vector)
            outs = outs if first else outs + ((scalars, scalars) if last else (vector,))
            return pl.pallas_call(
                lambda *refs: step_kernel(side, first, last, *refs),
                out_shape=outs,
                in_specs=[SMEM, SMEM, VMEM, VMEM, VMEM, wide, wide] + [VMEM] * len(states),
                out_specs=tuple(VMEM for _ in outs),
                scratch_shapes=[
                    pltpu.VMEM(half_shape, BF16),
                    pltpu.VMEM(half_shape, BF16),
                    pltpu.VMEM(half_shape, F32),
                ]
                + copied,
                compiler_params=limit,
            )(listed, total, near(gram), near(own), near(other), keep(dense), keep(pairs), *(near(v) for v in states))

        started = [begin(side) for side in range(sides)]
        states = [(start,) for start, _ in started]
        values = [terms for _, terms in started]
        for count in range(ITERS):
            for side in range(sides):
                results = advance(side, count, values[side], states[side])
                if count == ITERS - 1:
                    iterate, direction, norms, values[side], squares = results
                    states[side] = (iterate, direction, norms, squares)
                elif count:
                    iterate, direction, residual, values[side] = results
                    states[side] = (iterate, residual, direction)
                else:
                    residual, values[side] = results
                    states[side] = (states[side][0], residual, residual)
        inputs = []
        for side in range(sides):
            inputs += [*states[side], *shared(values[side])]
        slice_rows = part // n_x
        solved, mine = pl.pallas_call(
            lambda *refs: finish_kernel(slice_rows, sides, *refs),
            out_shape=(pltpu.VMEM((part, K), F32), pltpu.VMEM((slice_rows, K), F32)),
            in_specs=[SMEM] + [VMEM] * len(inputs),
            out_specs=(VMEM, VMEM),
            compiler_params=limit,
            name="finish",
        )(place, *(near(v) for v in inputs))

        sources, pieces = [], []
        for mask_z, piece in enumerate(direct_z(mine)):
            if mask_z:
                for mask_x in range(n_x):
                    sources.append((mask_z, mask_x))
                    pieces.append(swap(piece, "col", mask_x) if mask_x else piece)
        return pl.pallas_call(
            lambda *refs: place_kernel(part, slice_rows, sources, *refs),
            out_shape=jax.ShapeDtypeStruct((user_rows, K), F32),
            in_specs=[SMEM] + [VMEM] * (1 + len(pieces)),
            out_specs=VMEM,
            compiler_params=limit,
            name="place",
        )(place, near(solved), *(near(v) for v in pieces))

    return shards


def solution(mesh):
    n_row, n_col = mesh.shape["row"], mesh.shape["col"]
    inner = make_shards(n_row, n_col)

    return jax.shard_map(
        inner,
        mesh=mesh,
        in_specs=(
            P("row", None),
            P(("row", "col"), None),
            P("row", "col", None, None),
            P("row", "col", None),
            P("row", "col", None),
            P("row", "col", None, None),
            P("row", "col", None, None),
            P("row", "col", None, None),
            P("row", "col"),
        ),
        out_specs=P("row", None),
        check_vma=False,
    )
```

```python
import jax
import jax.numpy as jnp
from jax import lax
from jax.experimental import pallas as pl
from jax.experimental.pallas import tpu as pltpu
from jax.sharding import PartitionSpec as P


K = 128
BLOCK = 128
ITERS = 3
CONFIDENCE_SCALE = 40.0
RIDGE = 0.5
EPSILON = 1e-06
GROUP_BITS = 3
GROUP = 1 << GROUP_BITS
RADIX = 1024.0
F32 = jnp.float32
BF16 = jnp.bfloat16
NT = (((1,), (1,)), ((), ()))
NN = (((1,), (0,)), ((), ()))


def halves(value):
    high = value.astype(BF16)
    return high, (value - high.astype(F32)).astype(BF16)


def dot(a, b, dims):
    return lax.dot_general(a, b, dims, preferred_element_type=F32)


def dot3(a, b_high, b_low):
    a_high, a_low = halves(a)
    return dot(a_high, b_high, NN) + dot(a_high, b_low, NN) + dot(a_low, b_high, NN)


def pair_scores(v_high, v_low, y_both):
    wide = dot(v_high, y_both, NT)
    return wide[:, :BLOCK] + wide[:, BLOCK:] + dot(v_low, y_both[:BLOCK], NT)


def pair_pull(weights, y_both):
    high, low = halves(weights)
    return dot(jnp.concatenate([high, high], axis=1), y_both, NN) + dot(low, y_both[:BLOCK], NN)


def decode(code):
    counts = jnp.floor(code * (1.0 / RADIX))
    return counts * CONFIDENCE_SCALE, code - counts * RADIX


def row_dot(a, b):
    high, low = halves(a * b)
    return dot(jnp.concatenate([high, low], axis=1), jnp.ones((2 * K, K), BF16), NN)


def row_sums(value):
    high, low = halves(value)
    return dot(jnp.ones((8, 2 * K), BF16), jnp.concatenate([high, low], axis=1), NT)[:1]


def build_kernel(tiles, part_blocks, owned, sides, sources, first, final, mine_ref, *rest):
    given, rest = rest[:sources], rest[sources:]
    list_ref, total_ref, dense_ref, index, spots, facts, entry_ref, buf, blank, sem, sem_e, sem_b = rest[-12:]
    rows = given[0].shape[0]
    fact_copies = [
        pltpu.make_async_copy(ref.at[pl.ds(3 * tiles, 8), pl.ds(0, BLOCK)], facts.at[s], sem_e.at[0, s])
        for s, ref in enumerate(given)
    ]
    entry_copies = [
        pltpu.make_async_copy(ref, entry_ref.at[pl.ds(s * rows, rows)], sem_e.at[1, s])
        for s, ref in enumerate(given)
    ]
    for copy in fact_copies + entry_copies:
        copy.start()
    begun = (jnp.int32(0), jnp.int32(0))
    if not first:
        list_in, total_in = rest[:2]
        begun = (total_in[0], total_in[1])

        def carry_over(i, carry):
            list_ref[i] = list_in[i]
            return carry

        lax.fori_loop(0, list_ref.shape[0], carry_over, 0, unroll=8)
    for copy in fact_copies:
        copy.wait()
    my_z, my_x, flip = mine_ref[0], mine_ref[1], mine_ref[2]
    owned_bits, part_bits = owned.bit_length() - 1, part_blocks.bit_length() - 1
    side_blocks = part_blocks // sides
    side_bits = side_blocks.bit_length() - 1
    last = list_ref.shape[0] // GROUP - 1

    def spot(k, side):
        back = ((last - (k >> GROUP_BITS)) << GROUP_BITS) | (k & (GROUP - 1))
        return jnp.where(side == 1, back, k)

    totals = begun
    for source in range(sources):

        def scan(t, n, source=source):
            user = facts[source, 0, t]
            item = facts[source, 1, t]
            side = (user >> side_bits) & (sides - 1)
            at = spot(jnp.where(side == 1, n[1], n[0]), side)
            k = n[0] + n[1] - begun[0] - begun[1]
            index[k] = source * rows + t
            spots[k] = at
            list_ref[at] = ((user & (side_blocks - 1)) << 16) | ((item & (owned - 1)) ^ flip)
            missed = ((item >> owned_bits) ^ my_x) | ((user >> part_bits) ^ my_z)
            hit = jnp.where(missed == 0, 1, 0).astype(jnp.int32)
            return n[0] + hit * (1 - side), n[1] + hit * side

        totals = lax.fori_loop(0, tiles, scan, totals, unroll=8)
    total_ref[0], total_ref[1] = totals
    found = totals[0] + totals[1] - begun[0] - begun[1]
    for extra in range(GROUP - 1):
        index[found + extra] = 0
    for copy in entry_copies:
        copy.wait()
    ids = lax.broadcasted_iota(jnp.int32, (BLOCK, entry_ref.shape[1]), 0)

    def out_copy(at, slot, u):
        return pltpu.make_async_copy(buf.at[slot, u], dense_ref.at[at], sem.at[slot, u])

    def step(j, carry):
        slot = j & 1

        @pl.when(j >= 2)
        def _():
            for u in range(GROUP):
                out_copy(0, slot, u).wait()

        for u in range(GROUP):
            base = index[j * GROUP + u]
            users = entry_ref[pl.ds(base, 1), :]
            items = entry_ref[pl.ds(base + tiles, 1), :]
            counts = entry_ref[pl.ds(base + 2 * tiles, 1), :].astype(F32)
            user_hot = jnp.where(ids == users, 1.0, 0.0).astype(BF16)
            hit = ids == items
            item_hot = jnp.where(hit, 1.0, 0.0).astype(BF16)
            count_hot = jnp.where(hit, counts, 0.0).astype(BF16)
            both = dot(user_hot, jnp.concatenate([item_hot, count_hot], axis=0), NT)
            buf[slot, u] = both[:, :BLOCK] + both[:, BLOCK:] * RADIX
        for u in range(GROUP):

            @pl.when(j * GROUP + u < found)
            def _():
                out_copy(spots[j * GROUP + u], slot, u).start()

        return carry

    steps = (found + (GROUP - 1)) >> GROUP_BITS
    lax.fori_loop(0, steps, step, 0)

    def blanks(act):
        for side in range(2):
            ceiling = ((totals[side] + (GROUP - 1)) >> GROUP_BITS) << GROUP_BITS
            for extra in range(GROUP - 1):
                k = totals[side] + extra

                @pl.when(k < ceiling)
                def _():
                    at = spot(k, side)
                    list_ref[at] = 0
                    act(pltpu.make_async_copy(blank, dense_ref.at[at], sem_b.at[side, extra]))

    if final:
        blank[...] = jnp.zeros_like(blank)
        blanks(lambda copy: copy.start())

    @pl.when(steps >= 2)
    def _():
        for u in range(GROUP):
            out_copy(0, steps & 1, u).wait()

    for u in range(GROUP):

        @pl.when((steps - 1) * GROUP + u < found)
        def _():
            @pl.when(steps >= 1)
            def _():
                out_copy(0, (steps - 1) & 1, u).wait()

    if final:
        blanks(lambda copy: copy.wait())


def own_chunk(ref, chunk):
    return ref.at[pl.ds(chunk * GROUP, GROUP)]


def read_chunk(ref, chunk, scratch):
    if not scratch:
        return own_chunk(ref, chunk)
    pltpu.sync_copy(own_chunk(ref, chunk), scratch[0])
    return scratch[0]


def near(value):
    return pltpu.with_memory_space_constraint(value, pltpu.VMEM)


def far(value):
    return pltpu.with_memory_space_constraint(value, pltpu.HBM)


def choose(value, low, high, act):
    if high - low == 1:
        act(low)
        return
    middle = (low + high) // 2

    @pl.when(value < middle)
    def _():
        choose(value, low, middle, act)

    @pl.when(value >= middle)
    def _():
        choose(value, middle, high, act)


def bring_kernel(list_ref, total_ref, dense_ref, kept_ref, sem):
    chunks = [(total_ref[side] + (GROUP - 1)) >> GROUP_BITS for side in range(2)]

    def dense_copy(j):
        chunk = jnp.where(j < chunks[0], j, list_ref.shape[0] // GROUP - 1 - (j - chunks[0]))
        return pltpu.make_async_copy(own_chunk(dense_ref, chunk), own_chunk(kept_ref, chunk), sem.at[j])

    def begin(j, carry):
        dense_copy(j).start()
        return carry

    def end(j, carry):
        dense_copy(j).wait()
        return carry

    lax.fori_loop(0, chunks[0] + chunks[1], begin, 0)
    lax.fori_loop(0, chunks[0] + chunks[1], end, 0)


def gather_kernel(owners, blocks, list_ref, total_ref, *rest):
    items = rest[:owners]
    pair_ref = rest[owners]
    buf = rest[owners + 1 :]
    front, back = (((total_ref[side] + (GROUP - 1)) >> GROUP_BITS) << GROUP_BITS for side in range(2))
    slots = list_ref.shape[0]

    def step(j, carry):
        at = jnp.where(j < front, j, slots - back + (j - front))
        where = list_ref[at] & 65535
        rows = pl.ds(pl.multiple_of((where & (blocks - 1)) * BLOCK, BLOCK), BLOCK)
        target = buf[0] if buf else pair_ref.at[at]

        def split(owner):
            high, low = halves(items[owner][rows, :])
            target[:BLOCK, :] = high
            target[BLOCK:, :] = low

        choose(where >> (blocks.bit_length() - 1), 0, owners, split)
        if buf:
            pltpu.sync_copy(target, pair_ref.at[at])
        return carry

    lax.fori_loop(0, front + back, step, 0)


def start_kernel(side, list_ref, total_ref, start_ref, dense_ref, pair_ref, out_ref, v_high, v_low, *copies):
    chunks = (total_ref[side] + (GROUP - 1)) >> GROUP_BITS
    end = list_ref.shape[0] // GROUP - 1
    high, low = halves(start_ref[...])
    v_high[...] = high.reshape(v_high.shape)
    v_low[...] = low.reshape(v_low.shape)
    out_ref[...] = jnp.zeros_like(out_ref)

    def step(j, carry):
        chunk = end - j if side else j
        dense = read_chunk(dense_ref, chunk, copies[:1])
        both = read_chunk(pair_ref, chunk, copies[1:])
        pulled = []
        for u in range(GROUP):
            block = list_ref[chunk * GROUP + u] >> 16
            y_both = both[u]
            fit, ones = decode(dense[u])
            scores = pair_scores(v_high[block], v_low[block], y_both)
            pulled.append((block, pair_pull(ones + fit * (1.0 - scores), y_both)))
        for block, value in pulled:
            out_ref[block] += value
        return carry

    lax.fori_loop(0, chunks, step, 0)


def as_column(row, eye):
    return jnp.sum(jnp.where(eye, row, 0.0), axis=1, keepdims=True)


def eye_mask():
    return lax.broadcasted_iota(jnp.int32, (BLOCK, BLOCK), 0) == lax.broadcasted_iota(
        jnp.int32, (BLOCK, BLOCK), 1
    )


def step_kernel(side, first, last, list_ref, total_ref, gram_ref, own_ref, other_ref, dense_ref, pair_ref, *rest):
    given = 1 if first else 3
    states = rest[:given]
    made = 2 if first else 5 if last else 4
    outs = rest[given : given + made]
    v_high, v_low, acc, *copies = rest[given + made :]
    shape3 = v_high.shape
    chunks = (total_ref[side] + (GROUP - 1)) >> GROUP_BITS
    end = list_ref.shape[0] // GROUP - 1
    summed = own_ref[...] + other_ref[...]
    gram_high, gram_low = halves(gram_ref[...])
    if first:
        start = states[0][...]
        direction = summed - dot3(start, gram_high, gram_low) - RIDGE * start
        outs[0][...] = direction
    else:
        iterate, residual, direction = (ref[...] for ref in states)
        image = summed + dot3(direction, gram_high, gram_low) + RIDGE * direction
        norm_now = row_dot(residual, residual)
        alpha = norm_now / (row_dot(direction, image) + EPSILON)
        iterate = iterate + alpha * direction
        residual = residual - alpha * image
        norm_next = row_dot(residual, residual)
        direction = residual + norm_next / (norm_now + EPSILON) * direction
        outs[0][...] = iterate
        outs[1][...] = direction
        if last:
            for b in range(shape3[0]):
                rows = slice(b * BLOCK, (b + 1) * BLOCK)
                outs[2][b : b + 1, :] = row_sums(residual[rows] * residual[rows])
                along = dot3(direction[rows], gram_high, gram_low) + RIDGE * direction[rows]
                outs[4][b : b + 1, :] = row_sums(direction[rows] * along)
        else:
            outs[2][...] = residual
    high, low = halves(direction)
    v_high[...] = high.reshape(shape3)
    v_low[...] = low.reshape(shape3)
    acc[...] = jnp.zeros_like(acc)

    def step(j, carry):
        chunk = end - j if side else j
        dense = read_chunk(dense_ref, chunk, copies[:1])
        both = read_chunk(pair_ref, chunk, copies[1:])
        pulled = []
        for u in range(GROUP):
            block = list_ref[chunk * GROUP + u] >> 16
            y_both = both[u]
            fit, _ = decode(dense[u])
            scores = pair_scores(v_high[block], v_low[block], y_both)
            weighted = fit * scores
            pulled.append((block, weighted * scores if last else pair_pull(weighted, y_both)))
        for block, value in pulled:
            acc[block] += value
        return carry

    lax.fori_loop(0, chunks, step, 0)
    if last:
        for b in range(shape3[0]):
            outs[3][b : b + 1, :] = row_sums(acc[b])
    else:
        outs[3 if not first else 1][...] = acc[...].reshape(own_ref.shape)


def finish_kernel(slice_rows, sides, place_ref, *rest):
    out_ref, mine_ref = rest[-2:]
    eye = eye_mask()
    done = 0
    for side in range(sides):
        iterate_ref, direction_ref, norm_ref, square_ref, own_ref, other_ref = rest[6 * side : 6 * side + 6]
        curve = own_ref[...] + other_ref[...] + square_ref[...]
        alpha = norm_ref[...] / (curve + EPSILON)
        for b in range(alpha.shape[0]):
            rows = pl.ds(b * BLOCK, BLOCK)
            out_ref[pl.ds(done, BLOCK), :] = (
                iterate_ref[rows, :] + as_column(alpha[b : b + 1, :], eye) * direction_ref[rows, :]
            )
            done += BLOCK
    mine_ref[...] = out_ref[pl.ds(pl.multiple_of(place_ref[1] * slice_rows, 8), slice_rows), :]


def place_kernel(part, slice_rows, sources, place_ref, own_ref, *rest):
    pieces = rest[: len(sources)]
    out_ref = rest[-1]
    z, x = place_ref[0], place_ref[1]
    out_ref[pl.ds(pl.multiple_of(z * part, 8), part), :] = own_ref[...]
    for (mask_z, mask_x), piece in zip(sources, pieces):
        at = (z ^ mask_z) * part + (x ^ mask_x) * slice_rows
        out_ref[pl.ds(pl.multiple_of(at, 8), slice_rows), :] = piece[...]


SMEM = pl.BlockSpec(memory_space=pltpu.SMEM)
VMEM = pl.BlockSpec(memory_space=pltpu.VMEM)
ANY = pl.BlockSpec(memory_space=pl.ANY)


def make_shards(n_row, n_col):
    n_x = 1 << ((n_col.bit_length() - 1) // 2)
    n_z = n_col // n_x

    def swap(value, axis, mask):
        count = n_row if axis == "row" else n_col
        return lax.ppermute(value, axis, [(i, i ^ mask) for i in range(count)])

    def hop(value, pairs):
        return lax.ppermute(value, "col", [(a * n_x + x, b * n_x + x) for a, b in pairs for x in range(n_x)])

    def direct_z(value):
        return [value] + [swap(value, "col", k * n_x) for k in range(1, n_z)]

    def gather_z(value):
        if n_z != 4:
            return direct_z(value)
        out, mid = [(1, 0), (2, 3)], [(1, 2), (2, 1)]
        near = swap(value, "col", n_x)
        centre = hop(value, mid)
        middle = hop(near, mid)
        ends = hop(centre, out)
        far = hop(middle, out)
        second = middle + ends
        third = far + centre
        return [value, near, second, third]

    def shards(
        user_factors,
        item_factors,
        fetch_list,
        tile_user,
        tile_slot,
        entry_row,
        entry_col,
        entry_count,
        tile_count,
    ):
        row = lax.axis_index("row")
        col = lax.axis_index("col")
        my_z, my_x = col // n_x, col % n_x
        user_rows = user_factors.shape[0]
        part = user_rows // n_z
        part_blocks = part // BLOCK
        sides = 2 if part_blocks % 2 == 0 else 1
        side_rows = part // sides
        side_blocks = part_blocks // sides
        blocks = item_factors.shape[0] // BLOCK
        users = tile_user[0, 0]
        slots = tile_slot[0, 0]
        tiles = users.shape[0]
        width = entry_row.shape[-1]

        fetched = fetch_list[0, 0]
        peers, cap = fetched.shape
        flat = fetched.reshape(1, -1)
        local = jnp.sum(
            jnp.where(slots[:, None] == jnp.arange(peers * cap, dtype=jnp.int32)[None, :], flat, 0), axis=1
        )
        alive = jnp.arange(tiles, dtype=jnp.int32) < tile_count[0, 0]
        owner = slots // cap
        owner_row, owner_z, owner_x = owner // n_col, owner % n_col // n_x, owner % n_x
        owned = n_row * n_z * blocks
        named = owner_x * owned + (owner_row * n_z + owner_z) * blocks + local
        facts = jnp.stack([users, jnp.where(alive, named, -1).astype(jnp.int32)])
        facts = jnp.pad(facts, ((0, 6), (0, width - tiles)))
        packed = jnp.concatenate([entry_row[0, 0], entry_col[0, 0], entry_count[0, 0], facts], axis=0)
        entries = gather_z(packed)
        entries += [swap(v, "col", k) for k in range(1, n_x) for v in entries]
        slots_all = n_col * tiles + GROUP
        resident = slots_all * BLOCK * K * 8 <= 40 << 20
        limit = pltpu.CompilerParams(vmem_limit_bytes=(8 if resident else 24) << 20)
        hold, keep = (pltpu.VMEM, near) if resident else (pltpu.HBM, far)
        wide = VMEM if resident else ANY
        copied = [] if resident else [pltpu.VMEM((GROUP, BLOCK, BLOCK), F32), pltpu.VMEM((GROUP, 2 * BLOCK, K), BF16)]
        place = jnp.stack([my_z, my_x, (row * n_z + my_z) * blocks]).astype(jnp.int32)

        groups = ((0, 1), (2,), (3,)) if n_z == 4 else (tuple(range(n_z)),)
        stages = [[v for i, v in enumerate(entries) if i % n_z in group] for group in groups]
        state = ()
        for count, stage in enumerate(stages):
            first, final = count == 0, count == len(stages) - 1
            stage_slots = len(stage) * tiles + GROUP
            state = pl.pallas_call(
                lambda *refs, stage=stage, first=first, final=final: build_kernel(
                    tiles, part_blocks, owned, sides, len(stage), first, final, *refs
                ),
                out_shape=(
                    jax.ShapeDtypeStruct((slots_all,), jnp.int32),
                    jax.ShapeDtypeStruct((2,), jnp.int32),
                    pltpu.HBM((slots_all, BLOCK, BLOCK), F32),
                ),
                in_specs=[SMEM] + [ANY] * len(stage) + ([] if first else [SMEM, SMEM, ANY]),
                out_specs=(SMEM, SMEM, ANY),
                input_output_aliases={} if first else {len(stage) + 3: 2},
                scratch_shapes=[
                    pltpu.SMEM((stage_slots,), jnp.int32),
                    pltpu.SMEM((stage_slots,), jnp.int32),
                    pltpu.SMEM((len(stage), 8, BLOCK), jnp.int32),
                    pltpu.VMEM((len(stage) * packed.shape[0], width), jnp.int32),
                    pltpu.VMEM((2, GROUP, BLOCK, BLOCK), F32),
                    pltpu.VMEM((BLOCK, BLOCK), F32),
                    pltpu.SemaphoreType.DMA((2, GROUP)),
                    pltpu.SemaphoreType.DMA((2, len(stage))),
                    pltpu.SemaphoreType.DMA((2, GROUP)),
                ],
                compiler_params=limit,
            )(place, *stage, *state)
            state = (state[0], state[1], far(state[2]))
        listed, total, dense = state

        along_z = gather_z(item_factors)
        by_y = [along_z]
        for m in range(1, n_row // 2):
            by_y.append([swap(v, "row", 2 * m) for v in along_z])
        held_items = []
        for group in by_y:
            held_items += [group, [swap(v, "row", 1) for v in group]]
        held_items = [v for group in held_items for v in group]
        gram = jnp.dot(
            item_factors.T, item_factors, precision=lax.Precision.HIGH, preferred_element_type=F32
        )
        for axis, count, mask in (("col", n_x, 1), ("row", n_row, 1), ("col", n_col, n_x)):
            while mask < count:
                gram = gram + swap(gram, axis, mask)
                mask *= 2

        if resident:
            dense = pl.pallas_call(
                bring_kernel,
                out_shape=pltpu.VMEM((slots_all, BLOCK, BLOCK), F32),
                in_specs=[SMEM, SMEM, ANY],
                out_specs=VMEM,
                scratch_shapes=[pltpu.SemaphoreType.DMA((slots_all // GROUP,))],
                compiler_params=limit,
                name="bring",
            )(listed, total, far(dense))
        pairs = pl.pallas_call(
            lambda *refs: gather_kernel(n_row * n_z, blocks, *refs),
            out_shape=hold((slots_all, 2 * BLOCK, K), BF16),
            in_specs=[SMEM, SMEM] + [VMEM] * len(held_items),
            out_specs=wide,
            scratch_shapes=[] if resident else [pltpu.VMEM((2 * BLOCK, K), BF16)],
            compiler_params=limit,
            name="gather",
        )(listed, total, *(near(v) for v in held_items))
        half_shape = (side_blocks, BLOCK, K)

        def begin(side):
            start = lax.dynamic_slice(user_factors, (my_z * part + side * side_rows, 0), (side_rows, K))
            terms = pl.pallas_call(
                lambda *refs: start_kernel(side, *refs),
                out_shape=pltpu.VMEM(half_shape, F32),
                in_specs=[SMEM, SMEM, VMEM, wide, wide],
                out_specs=VMEM,
                scratch_shapes=[pltpu.VMEM(half_shape, BF16), pltpu.VMEM(half_shape, BF16)] + copied,
                compiler_params=limit,
            )(listed, total, near(start), keep(dense), keep(pairs))
            return start, terms.reshape(side_rows, K)

        def shared(value):
            others = [swap(value, "col", k) for k in range(1, n_x)]
            if n_x == 2:
                return value, others[0]
            stacked = jnp.take(jnp.stack([value] + others), my_x ^ jnp.arange(n_x), axis=0)
            return jnp.sum(stacked, axis=0), jnp.zeros_like(value)

        vector = pltpu.VMEM((side_rows, K), F32)
        scalars = pltpu.VMEM((side_blocks, BLOCK), F32)

        def advance(side, count, value, states):
            first, last = count == 0, count == ITERS - 1
            own, other = shared(value)
            outs = (vector, vector) if first else (vector, vector, scalars if last else vector)
            outs = outs if first else outs + ((scalars, scalars) if last else (vector,))
            return pl.pallas_call(
                lambda *refs: step_kernel(side, first, last, *refs),
                out_shape=outs,
                in_specs=[SMEM, SMEM, VMEM, VMEM, VMEM, wide, wide] + [VMEM] * len(states),
                out_specs=tuple(VMEM for _ in outs),
                scratch_shapes=[
                    pltpu.VMEM(half_shape, BF16),
                    pltpu.VMEM(half_shape, BF16),
                    pltpu.VMEM(half_shape, F32),
                ]
                + copied,
                compiler_params=limit,
            )(listed, total, near(gram), near(own), near(other), keep(dense), keep(pairs), *(near(v) for v in states))

        started = [begin(side) for side in range(sides)]
        states = [(start,) for start, _ in started]
        values = [terms for _, terms in started]
        for count in range(ITERS):
            for side in range(sides):
                results = advance(side, count, values[side], states[side])
                if count == ITERS - 1:
                    iterate, direction, norms, values[side], squares = results
                    states[side] = (iterate, direction, norms, squares)
                elif count:
                    iterate, direction, residual, values[side] = results
                    states[side] = (iterate, residual, direction)
                else:
                    residual, values[side] = results
                    states[side] = (states[side][0], residual, residual)
        inputs = []
        for side in range(sides):
            inputs += [*states[side], *shared(values[side])]
        slice_rows = part // n_x
        solved, mine = pl.pallas_call(
            lambda *refs: finish_kernel(slice_rows, sides, *refs),
            out_shape=(pltpu.VMEM((part, K), F32), pltpu.VMEM((slice_rows, K), F32)),
            in_specs=[SMEM] + [VMEM] * len(inputs),
            out_specs=(VMEM, VMEM),
            compiler_params=limit,
            name="finish",
        )(place, *(near(v) for v in inputs))

        sources, pieces = [], []
        for mask_z, piece in enumerate(direct_z(mine)):
            if mask_z:
                for mask_x in range(n_x):
                    sources.append((mask_z, mask_x))
                    pieces.append(swap(piece, "col", mask_x) if mask_x else piece)
        return pl.pallas_call(
            lambda *refs: place_kernel(part, slice_rows, sources, *refs),
            out_shape=jax.ShapeDtypeStruct((user_rows, K), F32),
            in_specs=[SMEM] + [VMEM] * (1 + len(pieces)),
            out_specs=VMEM,
            compiler_params=limit,
            name="place",
        )(place, near(solved), *(near(v) for v in pieces))

    return shards


def solution(mesh):
    n_row, n_col = mesh.shape["row"], mesh.shape["col"]
    inner = make_shards(n_row, n_col)

    return jax.shard_map(
        inner,
        mesh=mesh,
        in_specs=(
            P("row", None),
            P(("row", "col"), None),
            P("row", "col", None, None),
            P("row", "col", None),
            P("row", "col", None),
            P("row", "col", None, None),
            P("row", "col", None, None),
            P("row", "col", None, None),
            P("row", "col"),
        ),
        out_specs=P("row", None),
        check_vma=False,
    )
```
